128 devices in a mesh: gx: 4 (over y), gy: 4 (over z_lo, core), ta: 8 (over x, z_hi).
Axes of the slice: x: 4, y: 4, z: 4 (z_hi: 2, z_lo: 2; z = z_hi * 2 + z_lo), core: 2. Of those that a mesh axis runs over, the one named last changes fastest.
Arguments:
- tokens: bfloat16 [4, 4, 16, 128, 512], P('gx', 'gy', 'ta'), may hold values from -6 to 6
- norm_gain: float32 [512], replicated, may hold values from 0.1 to 1.9
- w_query: bfloat16 [512, 512], replicated, may hold values from -0.25 to 0.25
- w_key: bfloat16 [512, 512], replicated, may hold values from -0.25 to 0.25
- w_value: bfloat16 [512, 512], replicated, may hold values from -0.25 to 0.25
- w_proj: bfloat16 [512, 512], replicated, may hold values from -0.25 to 0.25
- temper: float32 [8], replicated, may hold values from 1 to 3
- neighbours: int32 [4, 4, 16, 27], P('gx', 'gy', 'ta'), may hold values from 0 to 255, as said below
- valid_mask: int32 [4, 4, 16, 27], P('gx', 'gy', 'ta'), may hold values from 0 to 1, as said below
- cotangent: bfloat16 [4, 4, 16, 128, 512], P('gx', 'gy', 'ta'), may hold values from -6 to 6
Outputs:
- layer_out: bfloat16 [4, 4, 16, 128, 512], P('gx', 'gy', 'ta')
- grad_tokens: float32 [4, 4, 16, 128, 512], P('gx', 'gy', 'ta')
- grad_gain: float32 [512], replicated
- grad_query: float32 [512, 512], replicated
- grad_key: float32 [512, 512], replicated
- grad_value: float32 [512, 512], replicated
- grad_proj: float32 [512, 512], replicated
- grad_temper: float32 [8], replicated
The draws below stay inside these ranges and needn't reach their ends.
Inputs may be any that keep to these rules, and one draw needn't show every extreme that they name: `neighbours`: row (a, b, c) names the 27 blocks (i, j, k) with i - a, j - b, k - c each in -1, 0, 1 modulo 4, 4, 16, each once, in any order; block (i, j, k) is numbered (i * 4 + j) * 16 + k. `valid_mask`: the entry that names the row's own block is 1.
All inputs are finite; a program needn't handle non-finite values.
Results may differ from the reference program's by a relative error of at most 0.013.
The reference program's roundings to bfloat16 on the way (of `hidden`, `value_n`, `probs_b`, `mixed` and `scaled`) count: a program that leaves them out, or rounds other values in their place, can miss the bound.
Values may be sent and summed in bfloat16 or wider, within the bound.
No kernel may reach another device: no remote copies, remote signals or barrier semaphores. Data moves between devices by JAX's collectives and lax.ppermute only.
A program may use at most 192 MiB of HBM per device.

```python
import math
import jax
import jax.numpy as jnp
from jax import lax

D = 512
H = 8
DH = 64
BLK = 128
NB = 27
BX = 4
BY = 4
BT = 16


def slot_order(key):
    base = jax.random.fold_in(key, 11)
    blocks = BX * BY * BT
    ranks = jax.random.randint(base, (blocks, NB), 0, 1 << 20) * 32 + jnp.arange(NB, dtype=jnp.int32)[None, :]
    return jnp.argsort(ranks, axis=1).astype(jnp.int32)


def draw_neighbours(key, part):
    order = slot_order(key)
    blocks = BX * BY * BT
    cells = jnp.arange(blocks, dtype=jnp.int32)
    along_x = cells // (BY * BT)
    along_y = cells // BT % BY
    along_t = cells % BT
    near_x = (along_x[:, None] + order // 9 - 1) % BX
    near_y = (along_y[:, None] + order // 3 % 3 - 1) % BY
    near_t = (along_t[:, None] + order % 3 - 1) % BT
    numbers = (near_x * BY + near_y) * BT + near_t
    return numbers.astype(jnp.int32).reshape(BX, BY, BT, NB)


def draw_valid_mask(key, part):
    order = slot_order(key)
    blocks = BX * BY * BT
    share = jax.random.randint(jax.random.fold_in(key, 12), (blocks, 1), 30, 101)
    rolled = jax.random.randint(jax.random.fold_in(key, 13), (blocks, NB), 0, 100)
    kept = jnp.logical_or(rolled < share, order == 13)
    return kept.astype(jnp.int32).reshape(BX, BY, BT, NB)


def shard_levels(key, extent, pieces, least, top_value):
    def one(position, shards_of):
        steps = jax.random.uniform(jax.random.fold_in(jax.random.fold_in(key, 6), position), (shards_of,), jnp.float32, least / len(pieces), top_value / len(pieces))
        return jnp.repeat(jnp.exp(steps), extent[position] // shards_of).reshape((-1,) + (1,) * (len(extent) - position - 1))

    level = one(*pieces[0])
    for cut in pieces[1:]:
        level = level * one(*cut)
    return level


def centred(stream_key, extent, width, bound, shards=(), kind=jnp.bfloat16):
    gain = shard_levels(stream_key, extent, shards, -0.22, 0.18) if shards else 1.0
    values = jax.random.normal(stream_key, extent, jnp.float32) * width * gain
    return jnp.minimum(jnp.maximum(values, -bound), bound).astype(kind)


def setup_inputs(seed: int = 0) -> dict:
    arg_keys = jax.random.split(jax.random.key(seed), 11)
    tokens = centred(arg_keys[0], (BX, BY, BT, BLK, D), 1.0, 6.0, ((0, 4), (1, 4), (2, 8)))
    norm_gain = jnp.clip(1.0 + 0.18 * jax.random.normal(arg_keys[1], (D,), jnp.float32), 0.1, 1.9)
    w_query = centred(arg_keys[2], (D, D), D ** -0.5, 0.25)
    w_key = centred(arg_keys[3], (D, D), D ** -0.5, 0.25)
    w_value = centred(arg_keys[4], (D, D), D ** -0.5, 0.25)
    w_proj = centred(arg_keys[5], (D, D), D ** -0.5, 0.25)
    temper = jnp.clip(jnp.exp(jax.random.uniform(arg_keys[6], (H,), jnp.float32, math.log(1.0), math.log(3.0))), 1.0, 3.0)
    neighbours = draw_neighbours(jax.random.fold_in(arg_keys[10], 71), 0)
    valid_mask = draw_valid_mask(jax.random.fold_in(arg_keys[10], 71), 0)
    cotangent = centred(arg_keys[9], (BX, BY, BT, BLK, D), 1.0, 6.0, ((0, 4), (1, 4), (2, 8)))
    return dict(tokens=tokens, norm_gain=norm_gain, w_query=w_query, w_key=w_key, w_value=w_value, w_proj=w_proj, temper=temper, neighbours=neighbours, valid_mask=valid_mask, cotangent=cotangent)


NORM_EPS = 1e-05
HEAD_EPS = 1e-06

def norm_rows(tokens):
    values = tokens.astype(jnp.float32)
    factor = lax.rsqrt(lax.optimization_barrier(jnp.mean(values * values, axis=-1, keepdims=True)) + NORM_EPS)
    return (values * factor, factor)

def norm_heads(joined, head_count):
    split_shape = joined.shape[:-1] + (head_count, joined.shape[-1] // head_count)
    shaped = joined.reshape(split_shape)
    factor = lax.rsqrt(lax.optimization_barrier(jnp.mean(shaped * shaped, axis=-1, keepdims=True)) + HEAD_EPS)
    return ((shaped * factor).reshape(joined.shape), factor)

def back_heads(normed, factor, upstream, head_count):
    split_shape = normed.shape[:-1] + (head_count, normed.shape[-1] // head_count)
    unit_rows = normed.reshape(split_shape)
    slope_rows = upstream.reshape(split_shape)
    result = factor * (slope_rows - unit_rows * lax.optimization_barrier(jnp.mean(unit_rows * slope_rows, axis=-1, keepdims=True)))
    return result.reshape(normed.shape)

def outer_sum(left_rows, right_rows):
    return lax.dot_general(left_rows, right_rows, (((0,), (0,)), ((), ())), preferred_element_type=jnp.float32)

def reference(tokens, norm_gain, w_query, w_key, w_value, w_proj, temper, neighbours, valid_mask, cotangent):
    blocks = BX * BY * BT
    score_scale = DH ** (-0.5)
    unit_in, factor = norm_rows(tokens)
    hidden = (unit_in * norm_gain).astype(jnp.bfloat16)
    query_f, query_factor = norm_heads(jnp.dot(hidden, w_query, preferred_element_type=jnp.float32), H)
    key_f, key_factor = norm_heads(jnp.dot(hidden, w_key, preferred_element_type=jnp.float32), H)
    query_n = query_f.astype(jnp.bfloat16)
    key_n = key_f.astype(jnp.bfloat16)
    value_n = jnp.dot(hidden, w_value, preferred_element_type=jnp.float32).astype(jnp.bfloat16)
    back_mixed = jnp.dot(cotangent, w_proj.T, preferred_element_type=jnp.float32).astype(jnp.bfloat16)
    key_rows = key_n.reshape(blocks, BLK, D)
    value_rows = value_n.reshape(blocks, BLK, D)
    temper_col = temper[:, None, None]

    def visit(accums, packed):
        key_acc, value_acc = accums
        query_blk, back_blk, block_ids, keep_row = packed
        gathered_k = key_rows[block_ids].reshape(NB * BLK, H, DH).astype(jnp.float32)
        gathered_v = value_rows[block_ids].reshape(NB * BLK, H, DH).astype(jnp.float32)
        query_h = query_blk.reshape(BLK, H, DH).astype(jnp.float32)
        back_h = back_blk.reshape(BLK, H, DH).astype(jnp.float32)
        key_keep = jnp.repeat(keep_row.astype(jnp.float32), BLK)
        scores = jnp.einsum('qhd,khd->hqk', query_h, gathered_k) * score_scale
        weights = jnp.exp(temper_col * scores) * key_keep
        totals = lax.optimization_barrier(jnp.sum(weights, axis=-1, keepdims=True))
        probs = weights / totals
        probs_b = lax.optimization_barrier(probs.astype(jnp.bfloat16)).astype(jnp.float32)
        mixed = jnp.einsum('hqk,khd->qhd', probs_b, gathered_v).reshape(BLK, D).astype(jnp.bfloat16)
        slopes = jnp.einsum('qhd,khd->hqk', back_h, gathered_v)
        inners = lax.optimization_barrier(jnp.sum(probs * slopes, axis=-1, keepdims=True))
        score_grad = probs * (slopes - inners)
        temper_part = lax.optimization_barrier(jnp.sum(score_grad * scores, axis=(1, 2)))
        scaled = lax.optimization_barrier((score_grad * (temper_col * score_scale)).astype(jnp.bfloat16)).astype(jnp.float32)
        query_grad = jnp.einsum('hqk,khd->qhd', scaled, gathered_k).reshape(BLK, D)
        key_part = jnp.einsum('hqk,qhd->khd', scaled, query_h).reshape(NB, BLK, D)
        value_part = jnp.einsum('hqk,qhd->khd', probs_b, back_h).reshape(NB, BLK, D)
        key_acc = key_acc.at[block_ids].add(key_part)
        value_acc = value_acc.at[block_ids].add(value_part)
        return ((key_acc, value_acc), (mixed, query_grad, temper_part))
    zeros_acc = jnp.zeros((blocks, BLK, D), jnp.float32)
    inputs_scan = (query_n.reshape(blocks, BLK, D), back_mixed.reshape(blocks, BLK, D), neighbours.reshape(blocks, NB).astype(jnp.int32), valid_mask.reshape(blocks, NB))
    (key_grad, value_grad), (mixed, query_grad, temper_parts) = lax.scan(visit, (zeros_acc, zeros_acc), inputs_scan)
    layer_out = jnp.dot(mixed, w_proj, preferred_element_type=jnp.float32).astype(jnp.bfloat16).reshape(tokens.shape)
    query_d = back_heads(query_f, query_factor, query_grad.reshape(tokens.shape), H).astype(jnp.bfloat16)
    key_d = back_heads(key_f, key_factor, key_grad.reshape(tokens.shape), H).astype(jnp.bfloat16)
    value_d = value_grad.reshape(tokens.shape).astype(jnp.bfloat16)
    hidden_rows = hidden.reshape(-1, D)
    grad_query = outer_sum(hidden_rows, query_d.reshape(-1, D))
    grad_key = outer_sum(hidden_rows, key_d.reshape(-1, D))
    grad_value = outer_sum(hidden_rows, value_d.reshape(-1, D))
    grad_proj = outer_sum(mixed.reshape(-1, D), cotangent.reshape(-1, D))
    back_hidden = jnp.dot(query_d, w_query.T, preferred_element_type=jnp.float32) + jnp.dot(key_d, w_key.T, preferred_element_type=jnp.float32) + jnp.dot(value_d, w_value.T, preferred_element_type=jnp.float32)
    slope_in = back_hidden * norm_gain
    grad_tokens = factor * (slope_in - unit_in * lax.optimization_barrier(jnp.mean(slope_in * unit_in, axis=-1, keepdims=True)))
    grad_gain = lax.optimization_barrier(jnp.sum((back_hidden * unit_in).reshape(-1, D), axis=0))
    grad_temper = lax.optimization_barrier(jnp.sum(temper_parts, axis=0))
    return (layer_out, grad_tokens, grad_gain, grad_query, grad_key, grad_value, grad_proj, grad_temper)
```

```python
import math

import jax
import jax.numpy as jnp
from jax import lax
from jax.experimental import pallas as pl
from jax.experimental.pallas import tpu as pltpu
from jax.sharding import Mesh, PartitionSpec as P

NORM_EPS = 1e-05
HEAD_EPS = 1e-06
D = 512
H = 8
DH = 64
BLK = 128
NB = 27
ROWS = 256
SCALE = DH**-0.5
BF = jnp.bfloat16
F32 = jnp.float32
ZLINE = ("zl", "cr", "zh")
PLANE = ("gx", "tx")
ALL = ("gx", "zl", "cr", "tx", "zh")
VMEM_LIMIT = 56 * 1024 * 1024


def params():
    return pltpu.CompilerParams(vmem_limit_bytes=VMEM_LIMIT)


def dot_nn(left, right):
    return jnp.dot(left, right, preferred_element_type=F32)


def dot_nt(left, right):
    return lax.dot_general(left, right, (((1,), (1,)), ((), ())), preferred_element_type=F32)


def dot_tn(left, right):
    return lax.dot_general(left, right, (((0,), (0,)), ((), ())), preferred_element_type=F32)


def head(values, index):
    return values[:, index * DH : (index + 1) * DH]


def normed_hidden(tok_ref, gain_ref):
    values = tok_ref[...].astype(F32)
    factor = lax.rsqrt(jnp.mean(values * values, axis=-1, keepdims=True) + NORM_EPS)
    unit = values * factor
    return unit, factor, (unit * gain_ref[...]).astype(BF)


def project_kernel(tok, gain, cot, keep, wq, wk, wv, wp, kv_out, qb_out, qf_out, kf_out):
    _, _, hidden = normed_hidden(tok, gain)
    key_f = dot_nn(hidden, wk[...])
    value = dot_nn(hidden, wv[...]).astype(BF)
    kf_out[...] = key_f
    for h in range(H):
        part = head(key_f, h)
        factor = lax.rsqrt(jnp.mean(part * part, axis=-1, keepdims=True) + HEAD_EPS)
        kv_out[h] = jnp.concatenate([(part * factor).astype(BF), head(value, h)], axis=1)
    query_f = dot_nn(hidden, wq[...])
    back = dot_nt(cot[...], wp[...]).astype(BF)
    qf_out[...] = query_f
    for h in range(H):
        part = head(query_f, h)
        factor = lax.rsqrt(jnp.mean(part * part, axis=-1, keepdims=True) + HEAD_EPS)
        qb_out[h, :ROWS] = jnp.concatenate([(part * factor).astype(BF), head(back, h)], axis=1)
        qb_out[h, ROWS:] = keep[...]


def attend_kernel(
    coef, keep, own, xm, xp, tm, tp, cmm, cmp, cpm, cpp, qb,
    mq_out, own_out, xm_out, xp_out, tm_out, tp_out, cmm_out, cmp_out, cpm_out, cpp_out,
    kvall, kvt, acc, wbuf, sems,
):
    moves = [
        (cmm, 0, 0), (xm, 0, None), (cmp, 0, 5),
        (tm, 1, 0), (own, 1, None), (tp, 1, 5),
        (cpm, 2, 0), (xp, 2, None), (cpp, 2, 5),
    ]
    copies = []
    for number, (src, dx, slot) in enumerate(moves):
        dst = kvall.at[dx, :, pl.ds(1, 4)] if slot is None else kvall.at[dx, :, slot]
        copies.append(pltpu.make_async_copy(src, dst, sems.at[number]))
    for copy in copies:
        copy.start()
    acc[...] = jnp.zeros_like(acc)
    for copy in copies:
        copy.wait()
    for dx in range(3):
        for y in range(4):
            for t in range(6):
                kvt[dx, y, :, t * BLK : (t + 1) * BLK] = kvall[dx, y, t].T

    exp_coef = coef[0]
    grad_coef = coef[1]
    lane = lax.broadcasted_iota(jnp.int32, (BLK, 2 * DH), 1)
    low = (lane < DH).astype(F32).astype(BF)
    high = (lane >= DH).astype(F32).astype(BF)

    def fold(values):
        return jnp.sum(values.reshape(-1, 8, BLK), axis=0)

    def one_block(number, carry):
        y = number // 4
        t = number % 4
        rows = pl.multiple_of((t % 2) * BLK, BLK)
        both = qb[y * 2 + t // 2, pl.ds(rows, BLK), :]
        spread = jnp.concatenate([both * low, both * high], axis=0)
        total = jnp.zeros((8, BLK), F32)
        inner = jnp.zeros((8, BLK), F32)
        for g in range(9):
            dx, dy = g // 3, g % 3
            yy = (y + dy + 3) % 4
            keys = kvall[dx, yy, pl.ds(t, 3)].reshape(3 * BLK, 2 * DH)
            pair = dot_nt(keys, spread)
            for k in range(3):
                score = pair[k * BLK : (k + 1) * BLK, :BLK]
                slope = pair[k * BLK : (k + 1) * BLK, BLK:]
                weight = jnp.exp2(score * exp_coef) * keep[number * NB + g * 3 + k]
                total = total + fold(weight)
                inner = inner + fold(weight * slope)
                base = (g * 3 + k) * BLK
                wbuf[base : base + BLK, :BLK] = weight
                wbuf[base : base + BLK, BLK:] = slope
        total_row = jnp.sum(total, axis=0, keepdims=True)
        inverse = 1.0 / total_row
        inner_row = jnp.sum(inner, axis=0, keepdims=True) * inverse
        out = jnp.zeros((2 * DH, 2 * BLK), F32)
        for g in range(9):
            dx, dy = g // 3, g % 3
            yy = (y + dy + 3) % 4
            base = g * 3 * BLK
            prob = wbuf[base : base + 3 * BLK, :BLK] * inverse
            slope = wbuf[base : base + 3 * BLK, BLK:]
            scaled = (prob * (slope - inner_row)) * grad_coef
            mixed = jnp.concatenate([scaled.astype(BF), prob.astype(BF)], axis=1)
            update = dot_nn(mixed, spread)
            acc[dx, yy, pl.ds(t, 3)] += update.reshape(3, BLK, 2 * DH)
            lanes = pl.multiple_of(t * BLK, BLK)
            out = out + dot_nn(kvt[dx, yy, :, pl.ds(lanes, 3 * BLK)], mixed)
        mq_out[number] = jnp.concatenate([out[DH:, BLK:].T, out[:DH, :BLK].T], axis=1).astype(BF)
        return carry

    lax.fori_loop(0, 16, one_block, 0)
    own_out[...] = acc[1, :, 1:5]
    for out_ref, dx in ((xm_out, 0), (xp_out, 2)):
        out_ref[...] = acc[dx, :, 1:5].astype(BF)
    for out_ref, dx, slot in (
        (tm_out, 1, 0), (tp_out, 1, 5), (cmm_out, 0, 0),
        (cmp_out, 0, 5), (cpm_out, 2, 0), (cpp_out, 2, 5),
    ):
        out_ref[...] = acc[dx, :, slot].astype(BF)


def gather_kernel(own, rx0, rx2, lo0, lo1, lo2, hi0, hi1, hi2, out):
    total = own[...] + rx0[...].astype(F32) + rx2[...].astype(F32)
    first = lo0[...].astype(F32) + lo1[...].astype(F32) + lo2[...].astype(F32)
    last = hi0[...].astype(F32) + hi1[...].astype(F32) + hi2[...].astype(F32)
    out[:, 1:3] = total[:, 1:3].astype(BF)
    out[:, 0] = (total[:, 0] + first).astype(BF)
    out[:, 3] = (total[:, 3] + last).astype(BF)


def finish_kernel(
    tok, gain, cot, mq, kv, qf, kf, wq, wk, wv, wp, layer_out, grad_tok, parts
):
    unit, factor_in, hidden = normed_hidden(tok, gain)
    mixed = jnp.concatenate([mq[h][:, :DH] for h in range(H)], axis=1)
    layer_out[...] = dot_nn(mixed, wp[...]).astype(BF)
    query_grad = jnp.concatenate([mq[h][:, DH:] for h in range(H)], axis=1)
    key_grad = jnp.concatenate([kv[h][:, :DH] for h in range(H)], axis=1)
    value_d = jnp.concatenate([kv[h][:, DH:] for h in range(H)], axis=1)

    def back(flat, upstream):
        pieces, units = [], []
        for h in range(H):
            part = head(flat, h)
            slope = head(upstream, h).astype(F32)
            factor = lax.rsqrt(jnp.mean(part * part, axis=-1, keepdims=True) + HEAD_EPS)
            normed = part * factor
            pieces.append(
                (slope - normed * jnp.mean(normed * slope, axis=-1, keepdims=True)) * factor
            )
            units.append(normed)
        return jnp.concatenate(pieces, axis=1).astype(BF), jnp.concatenate(units, axis=1)

    query_d, query_n = back(qf[...], query_grad)
    key_d, _ = back(kf[...], key_grad)
    temper_part = jnp.sum(
        query_n.astype(BF).astype(F32) * query_grad.astype(F32), axis=0, keepdims=True
    )
    back_hidden = dot_nt(query_d, wq[...]) + dot_nt(key_d, wk[...]) + dot_nt(value_d, wv[...])
    slope_in = back_hidden * gain[...]
    grad_tok[...] = factor_in * (
        slope_in - unit * jnp.mean(slope_in * unit, axis=-1, keepdims=True)
    )
    gain_part = jnp.sum(back_hidden * unit, axis=0, keepdims=True)
    extras = jnp.concatenate(
        [gain_part[:, c * 128 : (c + 1) * 128] for c in range(4)]
        + [temper_part[:, c * 128 : (c + 1) * 128] for c in range(4)],
        axis=0,
    )
    parts[:, 64:72] = jnp.broadcast_to(extras.astype(BF)[None], (128, 8, 128))
    left = (hidden, hidden, hidden, mixed)
    right = (query_d, key_d, value_d, cot[...])
    for w in range(4):
        grad = dot_tn(left[w], right[w]).astype(BF)
        for c in range(4):
            parts[w * 32 : (w + 1) * 32, c * 16 : (c + 1) * 16] = grad[
                :, c * 128 : (c + 1) * 128
            ].reshape(32, 16, 128)


def whole(shape, dtype):
    return jax.ShapeDtypeStruct(shape, dtype)


def exchange(block, dx, dt):
    pairs = [
        (a * 4 + b, ((a + dx) % 4) * 4 + (b + dt) % 4) for a in range(4) for b in range(4)
    ]
    return lax.ppermute(block, PLANE, pairs)


def local(
    tokens, norm_gain, w_query, w_key, w_value, w_proj, temper, neighbours, valid_mask, cotangent
):
    tok = tokens.reshape(ROWS, D)
    cot = cotangent.reshape(ROWS, D)
    gain = norm_gain.reshape(1, D)
    place_x = lax.axis_index("gx")
    place_y = lax.axis_index("zl") * 2 + lax.axis_index("cr")
    place_t = (lax.axis_index("tx") * 2 + lax.axis_index("zh")) * 2 + jnp.arange(2)[:, None]
    ids = neighbours.reshape(2, NB)
    step_t = (ids % 16 - place_t + 1) % 16
    step_y = (ids // 16 % 4 - place_y + 1) % 4
    step_x = (ids // 64 - place_x + 1) % 4
    slots = step_x * 9 + step_y * 3 + step_t
    kept = jnp.sum(
        jnp.where(
            slots[:, :, None] == jnp.arange(128)[None, None, :],
            valid_mask.reshape(2, NB)[:, :, None],
            0,
        ),
        axis=1,
    )
    keep_rows = jnp.pad(kept.astype(BF), ((0, 14), (0, 0)))

    kv_send, qb_send, query_f, key_f = pl.pallas_call(
        project_kernel,
        out_shape=(
            whole((H, ROWS, 2 * DH), BF),
            whole((H, ROWS + 16, 2 * DH), BF),
            whole((ROWS, D), F32),
            whole((ROWS, D), F32),
        ),
        compiler_params=params(),
    )(tok, gain, cot, keep_rows, w_query, w_key, w_value, w_proj)

    own = lax.all_to_all(kv_send, ZLINE, 0, 0, tiled=True).reshape(4, 4, BLK, 2 * DH)
    late, early = own[:, 3], own[:, 0]
    xm = exchange(own, 1, 0)
    xp = exchange(own, -1, 0)
    tm = exchange(late, 0, 1)
    tp = exchange(early, 0, -1)
    cmm = exchange(late, 1, 1)
    cmp = exchange(early, 1, -1)
    cpm = exchange(late, -1, 1)
    cpp = exchange(early, -1, -1)
    qb = lax.all_to_all(qb_send, ZLINE, 0, 0, tiled=True)
    keep = qb[:, ROWS : ROWS + 2, :NB].astype(F32).reshape(16 * NB)
    head_id = (lax.axis_index("zl") * 2 + lax.axis_index("cr")) * 2 + lax.axis_index("zh")
    temp = temper[head_id] * SCALE
    coef = jnp.stack([temp * math.log2(math.e), temp])

    any_spec = pl.BlockSpec(memory_space=pl.ANY)
    smem = pl.BlockSpec(memory_space=pltpu.SMEM)
    vmem = pl.BlockSpec(memory_space=pltpu.VMEM)
    full = (4, 4, BLK, 2 * DH)
    edge = (4, BLK, 2 * DH)
    outs = pl.pallas_call(
        attend_kernel,
        out_shape=(
            whole((16, BLK, 2 * DH), BF), whole(full, F32), whole(full, BF), whole(full, BF),
        ) + tuple(whole(edge, BF) for _ in range(6)),
        in_specs=[smem, smem] + [any_spec] * 9 + [vmem],
        out_specs=tuple([vmem] * 10),
        scratch_shapes=[
            pltpu.VMEM((3, 4, 6, BLK, 2 * DH), BF),
            pltpu.VMEM((3, 4, 2 * DH, 6 * BLK), BF),
            pltpu.VMEM((3, 4, 6, BLK, 2 * DH), F32),
            pltpu.VMEM((NB * BLK, 2 * BLK), F32),
            pltpu.SemaphoreType.DMA((9,)),
        ],
        compiler_params=params(),
    )(coef, keep, own, xm, xp, tm, tp, cmm, cmp, cpm, cpp, qb)
    mq_send, own_grad, gxm, gxp, gtm, gtp, gmm, gmp, gpm, gpp = outs
    rx0 = exchange(gxm, -1, 0)
    rx2 = exchange(gxp, 1, 0)
    hi0 = exchange(gtm, 0, -1)
    lo0 = exchange(gtp, 0, 1)
    hi1 = exchange(gmm, -1, -1)
    lo1 = exchange(gmp, -1, 1)
    hi2 = exchange(gpm, 1, -1)
    lo2 = exchange(gpp, 1, 1)
    mq = lax.all_to_all(mq_send.reshape(H, ROWS, 2 * DH), ZLINE, 0, 0, tiled=True)
    kv_grad = pl.pallas_call(
        gather_kernel, out_shape=whole(full, BF), compiler_params=params()
    )(own_grad, rx0, rx2, lo0, lo1, lo2, hi0, hi1, hi2)
    kv = lax.all_to_all(kv_grad.reshape(H, ROWS, 2 * DH), ZLINE, 0, 0, tiled=True)

    layer_out, grad_tokens, parts = pl.pallas_call(
        finish_kernel,
        out_shape=(whole((ROWS, D), BF), whole((ROWS, D), F32), whole((128, 72, 128), BF)),
        compiler_params=params(),
    )(tok, gain, cot, mq, kv, query_f, key_f, w_query, w_key, w_value, w_proj)

    arrived = lax.all_to_all(parts, ALL, 0, 0, tiled=True)
    summed = jnp.sum(arrived.astype(F32), axis=0)
    grad_gain = summed[64:68].reshape(D)
    grad_temper = jnp.sum(summed[68:72].reshape(H, DH), axis=1) / temper
    share = jnp.broadcast_to(summed[:64].astype(BF)[None], (128, 64, 128))
    shares = lax.all_to_all(share, ALL, 0, 0, tiled=True)
    grads = jnp.transpose(shares.reshape(4, 32, 4, 16, 128), (0, 1, 3, 2, 4))
    grads = grads.reshape(4, D, D).astype(F32)
    return (
        layer_out.reshape(tokens.shape),
        grad_tokens.reshape(tokens.shape),
        grad_gain,
        grads[0],
        grads[1],
        grads[2],
        grads[3],
        grad_temper,
    )


def solution(mesh):
    fine = Mesh(mesh.devices.reshape(4, 2, 2, 4, 2), ALL)
    lattice = ("gx", ("zl", "cr"), ("tx", "zh"))
    blocks = P(*lattice, None, None)
    lists = P(*lattice, None)
    return jax.shard_map(
        local,
        mesh=fine,
        in_specs=(blocks, P(), P(), P(), P(), P(), P(), lists, lists, blocks),
        out_specs=(blocks, blocks, P(), P(), P(), P(), P(), P()),
        check_vma=False,
    )
```

```python
import math

import jax
import jax.numpy as jnp
from jax import lax
from jax.experimental import pallas as pl
from jax.experimental.pallas import tpu as pltpu
from jax.sharding import Mesh, PartitionSpec as P

NORM_EPS = 1e-05
HEAD_EPS = 1e-06
D = 512
H = 8
DH = 64
BLK = 128
NB = 27
ROWS = 256
SCALE = DH**-0.5
BF = jnp.bfloat16
F32 = jnp.float32
ZLINE = ("zl", "cr", "zh")
PLANE = ("gx", "tx")
CORES = ("gx", "zl", "tx", "zh")
ALL = ("gx", "zl", "cr", "tx", "zh")
VMEM_LIMIT = 56 * 1024 * 1024


def params():
    return pltpu.CompilerParams(vmem_limit_bytes=VMEM_LIMIT)


def dot_nn(left, right):
    return jnp.dot(left, right, preferred_element_type=F32)


def dot_nt(left, right):
    return lax.dot_general(left, right, (((1,), (1,)), ((), ())), preferred_element_type=F32)


def dot_tn(left, right):
    return lax.dot_general(left, right, (((0,), (0,)), ((), ())), preferred_element_type=F32)


def head(values, index):
    return values[:, index * DH : (index + 1) * DH]


def normed_hidden(tokens, gain):
    values = tokens.astype(F32)
    factor = lax.rsqrt(jnp.mean(values * values, axis=-1, keepdims=True) + NORM_EPS)
    unit = values * factor
    return unit, factor, (unit * gain).astype(BF)


def high_low(values):
    upper = values.astype(BF).astype(F32)
    return upper, values - upper


def project_kernel(
    place, tok, gain, cot, neighbours, valid, wq, wk, wv, wp, kv_out, qb_out
):
    _, _, hidden = normed_hidden(tok[...], gain[...])
    lane = lax.broadcasted_iota(jnp.int32, (ROWS, 128), 1)
    factors = jnp.zeros((ROWS, 128), F32)
    key_f = dot_nn(hidden, wk[...])
    value = dot_nn(hidden, wv[...]).astype(BF)
    for h in range(H):
        part = head(key_f, h)
        factor = lax.rsqrt(jnp.mean(part * part, axis=-1, keepdims=True) + HEAD_EPS)
        factors = jnp.where(lane == H + h, factor, factors)
        kv_out[h] = jnp.concatenate([(part * factor).astype(BF), head(value, h)], axis=1)
    query_f = dot_nn(hidden, wq[...])
    back = dot_nt(cot[...], wp[...]).astype(BF)
    for h in range(H):
        part = head(query_f, h)
        factor = lax.rsqrt(jnp.mean(part * part, axis=-1, keepdims=True) + HEAD_EPS)
        factors = jnp.where(lane == h, factor, factors)
        qb_out[h, :ROWS] = jnp.concatenate([(part * factor).astype(BF), head(back, h)], axis=1)
    ids = neighbours[...]
    keep = valid[...]
    own_t = place[2] + lax.broadcasted_iota(jnp.int32, (2, NB), 0)
    step_t = jnp.bitwise_and(ids - own_t + 1, 15)
    step_y = jnp.bitwise_and(jnp.right_shift(ids, 4) - place[1] + 1, 3)
    step_x = jnp.bitwise_and(jnp.right_shift(ids, 6) - place[0] + 1, 3)
    slots = step_x * 9 + step_y * 3 + step_t
    short = lax.broadcasted_iota(jnp.int32, (2, 128), 1)
    kept = jnp.zeros((2, 128), F32)
    for slot in range(NB):
        hit = short == slots[:, slot : slot + 1]
        kept = kept + jnp.where(hit, keep[:, slot : slot + 1].astype(F32), 0.0)
    turned = factors.T
    for h in range(H):
        rows = [kept]
        for which in (h, H + h):
            line = turned[which : which + 1]
            for piece in high_low(line):
                rows += [piece[:, :BLK], piece[:, BLK:]]
        rows.append(jnp.zeros((6, 128), F32))
        qb_out[h, ROWS:] = jnp.concatenate(rows, axis=0).astype(BF)


def factor_rows(extra, base, which):
    first = extra[base : base + 1] + extra[base + 2 : base + 3]
    second = extra[base + 1 : base + 2] + extra[base + 3 : base + 4]
    return jnp.where(which == 0, first, second)


def attend_kernel(
    coef, keep, own, xm, xp, tm, tp, cmm, cmp, cpm, cpp, qb,
    mq_out, mqt_out, own_out, xm_out, xp_out, tm_out, tp_out, cmm_out, cmp_out, cpm_out, cpp_out,
    kvall, kvt, acc, wbuf, sems,
):
    moves = [
        (cmm, 0, 0), (xm, 0, None), (cmp, 0, 5),
        (tm, 1, 0), (own, 1, None), (tp, 1, 5),
        (cpm, 2, 0), (xp, 2, None), (cpp, 2, 5),
    ]
    copies = []
    for number, (src, dx, slot) in enumerate(moves):
        dst = kvall.at[dx, :, pl.ds(1, 4)] if slot is None else kvall.at[dx, :, slot]
        copies.append(pltpu.make_async_copy(src, dst, sems.at[number]))
    for copy in copies:
        copy.start()
    acc[...] = jnp.zeros_like(acc)
    for copy in copies:
        copy.wait()
    for dx in range(3):
        for y in range(4):
            for t in range(6):
                kvt[dx, y, :, t * BLK : (t + 1) * BLK] = kvall[dx, y, t].T

    exp_coef = coef[0]
    grad_coef = coef[1]
    lane = lax.broadcasted_iota(jnp.int32, (BLK, 2 * DH), 1)
    low = (lane < DH).astype(F32).astype(BF)
    high = (lane >= DH).astype(F32).astype(BF)

    def fold(values):
        return jnp.sum(values.reshape(-1, 8, BLK), axis=0)

    def one_block(number, carry):
        y = number // 4
        t = number % 4
        rows = pl.multiple_of((t % 2) * BLK, BLK)
        both = qb[y * 2 + t // 2, pl.ds(rows, BLK), :]
        spread = jnp.concatenate([both * low, both * high], axis=0)
        total = jnp.zeros((8, BLK), F32)
        inner = jnp.zeros((8, BLK), F32)
        for g in range(9):
            dx, dy = g // 3, g % 3
            yy = (y + dy + 3) % 4
            keys = kvall[dx, yy, pl.ds(t, 3)].reshape(3 * BLK, 2 * DH)
            pair = dot_nt(keys, spread)
            for k in range(3):
                score = pair[k * BLK : (k + 1) * BLK, :BLK]
                slope = pair[k * BLK : (k + 1) * BLK, BLK:]
                weight = jnp.exp2(score * exp_coef) * keep[number * NB + g * 3 + k]
                total = total + fold(weight)
                inner = inner + fold(weight * slope)
                base = (g * 3 + k) * BLK
                wbuf[base : base + BLK, :BLK] = weight
                wbuf[base : base + BLK, BLK:] = slope
        total_row = jnp.sum(total, axis=0, keepdims=True)
        inverse = 1.0 / total_row
        inner_row = jnp.sum(inner, axis=0, keepdims=True) * inverse
        out = jnp.zeros((2 * DH, 2 * BLK), F32)
        for g in range(9):
            dx, dy = g // 3, g % 3
            yy = (y + dy + 3) % 4
            base = g * 3 * BLK
            prob = wbuf[base : base + 3 * BLK, :BLK] * inverse
            slope = wbuf[base : base + 3 * BLK, BLK:]
            scaled = (prob * (slope - inner_row)) * grad_coef
            mixed = jnp.concatenate([scaled.astype(BF), prob.astype(BF)], axis=1)
            update = dot_nn(mixed, spread)
            acc[dx, yy, pl.ds(t, 3)] += update.reshape(3, BLK, 2 * DH)
            lanes = pl.multiple_of(t * BLK, BLK)
            out = out + dot_nn(kvt[dx, yy, :, pl.ds(lanes, 3 * BLK)], mixed)
        extra = qb[y * 2 + t // 2, ROWS:, :].astype(F32)
        factor = factor_rows(extra, 2, t % 2)
        query_t = both.astype(F32).T[:DH]
        grad_t = out[:DH, :BLK]
        inside = jnp.sum(query_t * grad_t, axis=0, keepdims=True)
        query_d = (grad_t - query_t * (inside * (1.0 / DH))) * factor
        joined = jnp.concatenate([out[DH:, BLK:], query_d], axis=0)
        mq_out[y * 2 + t // 2, pl.ds(rows, BLK), :] = joined.T.astype(BF)
        mqt_out[number] = joined.astype(BF)
        return carry + inside

    inside = lax.fori_loop(0, 16, one_block, jnp.zeros((1, BLK), F32))
    upper, lower = high_low(jnp.broadcast_to(jnp.sum(inside, axis=1, keepdims=True), (1, BLK)))
    tail = jnp.concatenate([upper, lower, jnp.zeros((14, BLK), F32)], axis=0).astype(BF)
    for chunk in range(H):
        mq_out[chunk, ROWS:, :] = tail
    own_out[...] = acc[1, :, 1:5]
    for out_ref, dx in ((xm_out, 0), (xp_out, 2)):
        out_ref[...] = acc[dx, :, 1:5].astype(BF)
    for out_ref, dx, slot in (
        (tm_out, 1, 0), (tp_out, 1, 5), (cmm_out, 0, 0),
        (cmp_out, 0, 5), (cpm_out, 2, 0), (cpp_out, 2, 5),
    ):
        out_ref[...] = acc[dx, :, slot].astype(BF)


def head_kernel(
    own, rx0, rx2, lo0, lo1, lo2, hi0, hi1, hi2, kv, qb, mqt, mq, tok, cot, gain,
    kv_out, parts_out, turned,
):
    for b in range(16):
        y, t = b // 4, b % 4
        total = own[y, t] + rx0[y, t].astype(F32) + rx2[y, t].astype(F32)
        if t == 0:
            total = total + lo0[y].astype(F32) + lo1[y].astype(F32) + lo2[y].astype(F32)
        if t == 3:
            total = total + hi0[y].astype(F32) + hi1[y].astype(F32) + hi2[y].astype(F32)
        total_t = total.T
        key_t = kv[y, t].astype(F32).T[:DH]
        extra = qb[y * 2 + t // 2, ROWS:, :].astype(F32)
        factor = factor_rows(extra, 6, t % 2)
        grad_t = total_t[:DH]
        inside = jnp.sum(key_t * grad_t, axis=0, keepdims=True) * (1.0 / DH)
        joined = jnp.concatenate([(grad_t - key_t * inside) * factor, total_t[DH:]], axis=0)
        turned[:, b * BLK : (b + 1) * BLK] = joined.astype(BF)
        kv_out[b] = joined.T.astype(BF)
    query_part = jnp.zeros((DH, D), F32)
    proj_part = jnp.zeros((DH, D), F32)
    both_part = jnp.zeros((2 * DH, D), F32)
    for c in range(4):
        lines = slice(c * 512, (c + 1) * 512)
        _, _, hidden = normed_hidden(tok[lines], gain[...])
        mixed_t = jnp.concatenate([mqt[c * 4 + k] for k in range(4)], axis=1)
        proj_part = proj_part + dot_nn(mixed_t[:DH], cot[lines])
        query_part = query_part + dot_nn(mixed_t[DH:], hidden)
        both_part = both_part + dot_nn(turned[:, lines], hidden)
    upper = jnp.concatenate([mq[h, ROWS : ROWS + 1].astype(F32) for h in range(H)], axis=0)
    lower = jnp.concatenate([mq[h, ROWS + 1 : ROWS + 2].astype(F32) for h in range(H)], axis=0)
    extra = jnp.concatenate([upper, lower, upper, lower], axis=1).astype(BF)
    joined = jnp.concatenate([query_part, both_part, proj_part], axis=0).astype(BF)
    for g in range(16):
        parts_out[g, :16] = joined[g * 16 : (g + 1) * 16]
        parts_out[g, 16:] = extra


def sum_kernel(arrived, share_out, temper_out):
    total = jnp.zeros((24, D), F32)
    for g in range(16):
        total = total + arrived[g].astype(F32)
    temper_out[...] = total[16:, :128] + total[16:, 128:256]
    share = total[:16].astype(BF)
    for k in range(64):
        share_out[k] = share


def output_kernel(core, near, far, gain, wq, wk, wv, gq, gk, gv, gp, gg, turned):
    for which, source in ((core[0], near), (1 - core[0], far)):
        for m in range(4):
            for zl in range(2):
                for tx in range(4):
                    for zh in range(2):
                        piece = source[m * 16 + zl * 8 + tx * 2 + zh]
                        start = pl.multiple_of(zl * 256 + which * 128 + zh * 64 + tx * 16, 16)
                        turned[m, pl.ds(start, 16), :] = piece
    gp[...] = turned[3].astype(F32)
    total = jnp.zeros((D, 1), F32)
    for m, (out, weight) in enumerate(((gq, wq), (gk, wk), (gv, wv))):
        value = turned[m].T.astype(F32)
        out[...] = value
        total = total + jnp.sum(value * weight[...].astype(F32), axis=1, keepdims=True)
    line = jnp.broadcast_to(total, (D, 128)).T
    gg[...] = line[:1] / gain[...]


def finish_kernel(tok, gain, mq, kv, wq, wk, wv, wp, layer_out, grad_tok):
    unit, factor_in, _ = normed_hidden(tok[...], gain[...])
    mixed = jnp.concatenate([mq[h, :ROWS, :DH] for h in range(H)], axis=1)
    layer_out[...] = dot_nn(mixed, wp[...]).astype(BF)
    query_d = jnp.concatenate([mq[h, :ROWS, DH:] for h in range(H)], axis=1)
    key_d = jnp.concatenate([kv[h][:, :DH] for h in range(H)], axis=1)
    value_d = jnp.concatenate([kv[h][:, DH:] for h in range(H)], axis=1)
    back_hidden = dot_nt(query_d, wq[...]) + dot_nt(key_d, wk[...]) + dot_nt(value_d, wv[...])
    slope_in = back_hidden * gain[...]
    grad_tok[...] = factor_in * (
        slope_in - unit * jnp.mean(slope_in * unit, axis=-1, keepdims=True)
    )


def whole(shape, dtype):
    return jax.ShapeDtypeStruct(shape, dtype)


def exchange(block, dx, dt):
    pairs = [
        (a * 4 + b, ((a + dx) % 4) * 4 + (b + dt) % 4) for a in range(4) for b in range(4)
    ]
    return lax.ppermute(block, PLANE, pairs)


def local(
    tokens, norm_gain, w_query, w_key, w_value, w_proj, temper, neighbours, valid_mask, cotangent
):
    tok = tokens.reshape(ROWS, D)
    cot = cotangent.reshape(ROWS, D)
    gain = norm_gain.reshape(1, D)
    tok_all = lax.all_gather(tok, ZLINE, axis=0, tiled=True)
    cot_all = lax.all_gather(cot, ZLINE, axis=0, tiled=True)
    core = lax.axis_index("cr")
    place = jnp.stack(
        [
            lax.axis_index("gx"),
            lax.axis_index("zl") * 2 + core,
            (lax.axis_index("tx") * 2 + lax.axis_index("zh")) * 2,
        ]
    )
    any_spec = pl.BlockSpec(memory_space=pl.ANY)
    smem = pl.BlockSpec(memory_space=pltpu.SMEM)
    vmem = pl.BlockSpec(memory_space=pltpu.VMEM)

    kv_send, qb_send = pl.pallas_call(
        project_kernel,
        out_shape=(whole((H, ROWS, 2 * DH), BF), whole((H, ROWS + 16, 2 * DH), BF)),
        in_specs=[smem] + [vmem] * 9,
        out_specs=(vmem, vmem),
        compiler_params=params(),
    )(
        place, tok, gain, cot, neighbours.reshape(2, NB), valid_mask.reshape(2, NB),
        w_query, w_key, w_value, w_proj,
    )

    own = lax.all_to_all(kv_send, ZLINE, 0, 0, tiled=True).reshape(4, 4, BLK, 2 * DH)
    late, early = own[:, 3], own[:, 0]
    xm = exchange(own, 1, 0)
    xp = exchange(own, -1, 0)
    tm = exchange(late, 0, 1)
    tp = exchange(early, 0, -1)
    cmm = exchange(late, 1, 1)
    cmp = exchange(early, 1, -1)
    cpm = exchange(late, -1, 1)
    cpp = exchange(early, -1, -1)
    qb = lax.all_to_all(qb_send, ZLINE, 0, 0, tiled=True)
    keep = qb[:, ROWS : ROWS + 2, :NB].astype(F32).reshape(16 * NB)
    head_id = (lax.axis_index("zl") * 2 + core) * 2 + lax.axis_index("zh")
    temp = temper[head_id] * SCALE
    coef = jnp.stack([temp * math.log2(math.e), temp])

    full = (4, 4, BLK, 2 * DH)
    edge = (4, BLK, 2 * DH)
    outs = pl.pallas_call(
        attend_kernel,
        out_shape=(
            whole((H, ROWS + 16, 2 * DH), BF), whole((16, 2 * DH, BLK), BF), whole(full, F32), whole(full, BF), whole(full, BF),
        ) + tuple(whole(edge, BF) for _ in range(6)),
        in_specs=[smem, smem] + [any_spec] * 9 + [vmem],
        out_specs=tuple([vmem] * 11),
        scratch_shapes=[
            pltpu.VMEM((3, 4, 6, BLK, 2 * DH), BF),
            pltpu.VMEM((3, 4, 2 * DH, 6 * BLK), BF),
            pltpu.VMEM((3, 4, 6, BLK, 2 * DH), F32),
            pltpu.VMEM((NB * BLK, 2 * BLK), F32),
            pltpu.SemaphoreType.DMA((9,)),
        ],
        compiler_params=params(),
    )(coef, keep, own, xm, xp, tm, tp, cmm, cmp, cpm, cpp, qb)
    mq_send, mqt, own_grad, gxm, gxp, gtm, gtp, gmm, gmp, gpm, gpp = outs
    rx0 = exchange(gxm, -1, 0)
    rx2 = exchange(gxp, 1, 0)
    hi0 = exchange(gtm, 0, -1)
    lo0 = exchange(gtp, 0, 1)
    hi1 = exchange(gmm, -1, -1)
    lo1 = exchange(gmp, -1, 1)
    hi2 = exchange(gpm, 1, -1)
    lo2 = exchange(gpp, 1, 1)
    mq = lax.all_to_all(mq_send, ZLINE, 0, 0, tiled=True)
    kv_back, parts = pl.pallas_call(
        head_kernel,
        out_shape=(whole((16, BLK, 2 * DH), BF), whole((16, 24, D), BF)),
        scratch_shapes=[pltpu.VMEM((2 * DH, 16 * BLK), BF)],
        compiler_params=params(),
    )(own_grad, rx0, rx2, lo0, lo1, lo2, hi0, hi1, hi2, own, qb, mqt, mq, tok_all, cot_all, gain)
    arrived = lax.all_to_all(parts, PLANE, 0, 0, tiled=True)
    kv = lax.all_to_all(kv_back.reshape(H, ROWS, 2 * DH), ZLINE, 0, 0, tiled=True)
    layer_out, grad_tokens = pl.pallas_call(
        finish_kernel,
        out_shape=(whole((ROWS, D), BF), whole((ROWS, D), F32)),
        compiler_params=params(),
    )(tok, gain, mq, kv, w_query, w_key, w_value, w_proj)
    share, temper_sum = pl.pallas_call(
        sum_kernel,
        out_shape=(whole((64, 16, D), BF), whole((H, 128), F32)),
        compiler_params=params(),
    )(arrived)
    near = lax.all_to_all(share, CORES, 0, 0, tiled=True)
    far = lax.ppermute(near, "cr", [(0, 1), (1, 0)])
    square = whole((D, D), F32)
    gq, gk, gv, gp, grad_gain = pl.pallas_call(
        output_kernel,
        out_shape=(square, square, square, square, whole((1, D), F32)),
        in_specs=[smem] + [vmem] * 6,
        scratch_shapes=[pltpu.VMEM((4, D, D), BF)],
        compiler_params=params(),
    )(core.reshape(1), near, far, gain, w_query, w_key, w_value)
    grad_temper = temper_sum[:, 0] / temper
    return (
        layer_out.reshape(tokens.shape),
        grad_tokens.reshape(tokens.shape),
        grad_gain.reshape(D),
        gq,
        gk,
        gv,
        gp,
        grad_temper,
    )


def solution(mesh):
    fine = Mesh(mesh.devices.reshape(4, 2, 2, 4, 2), ALL)
    lattice = ("gx", ("zl", "cr"), ("tx", "zh"))
    blocks = P(*lattice, None, None)
    lists = P(*lattice, None)
    return jax.shard_map(
        local,
        mesh=fine,
        in_specs=(blocks, P(), P(), P(), P(), P(), P(), lists, lists, blocks),
        out_specs=(blocks, blocks, P(), P(), P(), P(), P(), P()),
        check_vma=False,
    )
```

```python
import math

import jax
import jax.numpy as jnp
from jax import lax
from jax.experimental import pallas as pl
from jax.experimental.pallas import tpu as pltpu
from jax.sharding import Mesh, PartitionSpec as P

NORM_EPS = 1e-05
HEAD_EPS = 1e-06
D = 512
H = 8
DH = 64
BLK = 128
NB = 27
ROWS = 256
SCALE = DH**-0.5
BF = jnp.bfloat16
F32 = jnp.float32
GROUP = ("gx", "zl", "cr")
RING = ("zl", "tx", "zh")
CHIPS = ("gx", "zl", "tx", "zh")
ALL = ("gx", "zl", "cr", "tx", "zh")
EXTRA = 8
VMEM_LIMIT = 56 * 1024 * 1024


def params():
    return pltpu.CompilerParams(vmem_limit_bytes=VMEM_LIMIT)


def cost(micros):
    return pl.CostEstimate(
        flops=int(micros * 1e9), bytes_accessed=int(micros * 1e6), transcendentals=0
    )


def dot_nn(left, right):
    return jnp.dot(left, right, preferred_element_type=F32)


def dot_nt(left, right):
    return lax.dot_general(left, right, (((1,), (1,)), ((), ())), preferred_element_type=F32)


def dot_tn(left, right):
    return lax.dot_general(left, right, (((0,), (0,)), ((), ())), preferred_element_type=F32)


def head(values, index):
    return values[:, index * DH : (index + 1) * DH]


def normed_hidden(tokens, gain):
    values = tokens.astype(F32)
    factor = lax.rsqrt(jnp.mean(values * values, axis=-1, keepdims=True) + NORM_EPS)
    unit = values * factor
    return unit, factor, (unit * gain).astype(BF)


def high_low(values):
    upper = values.astype(BF).astype(F32)
    return upper, values - upper


def seat(h, slot):
    return (h // 2) * 4 + slot * 2 + h % 2


def project_kernel(
    place, tok, gain, cot, neighbours, valid, wq, wk, wv, wp, kv_out, qb_out, rows_out
):
    _, _, hidden = normed_hidden(tok[...], gain[...])
    for k in range(8):
        lines = slice((k % 2) * BLK, (k % 2 + 1) * BLK)
        rows_out[k, :, :D] = hidden[lines]
        rows_out[k, :, D:] = cot[lines]
    lane = lax.broadcasted_iota(jnp.int32, (ROWS, 128), 1)
    factors = jnp.zeros((ROWS, 128), F32)
    key_f = dot_nn(hidden, wk[...])
    value = dot_nn(hidden, wv[...]).astype(BF)
    for h in range(H):
        part = head(key_f, h)
        factor = lax.rsqrt(jnp.mean(part * part, axis=-1, keepdims=True) + HEAD_EPS)
        factors = jnp.where(lane == H + h, factor, factors)
        joined = jnp.concatenate([(part * factor).astype(BF), head(value, h)], axis=1)
        kv_out[seat(h, 0)] = joined[:BLK]
        kv_out[seat(h, 1)] = joined[BLK:]
    query_f = dot_nn(hidden, wq[...])
    back = dot_nt(cot[...], wp[...]).astype(BF)
    for h in range(H):
        part = head(query_f, h)
        factor = lax.rsqrt(jnp.mean(part * part, axis=-1, keepdims=True) + HEAD_EPS)
        factors = jnp.where(lane == h, factor, factors)
        joined = jnp.concatenate([(part * factor).astype(BF), head(back, h)], axis=1)
        qb_out[seat(h, 0), :BLK] = joined[:BLK]
        qb_out[seat(h, 1), :BLK] = joined[BLK:]
    ids = neighbours[...]
    keep = valid[...]
    own_t = place[2] + lax.broadcasted_iota(jnp.int32, (2, NB), 0)
    step_t = jnp.bitwise_and(ids - own_t + 1, 15)
    step_y = jnp.bitwise_and(jnp.right_shift(ids, 4) - place[1] + 1, 3)
    step_x = jnp.bitwise_and(jnp.right_shift(ids, 6) - place[0] + 1, 3)
    slots = step_x * 9 + step_y * 3 + step_t
    short = lax.broadcasted_iota(jnp.int32, (2, 128), 1)
    kept = jnp.zeros((2, 128), F32)
    for slot in range(NB):
        hit = short == slots[:, slot : slot + 1]
        kept = kept + jnp.where(hit, keep[:, slot : slot + 1].astype(F32), 0.0)
    turned = factors.T
    for h in range(H):
        for slot in range(2):
            lanes = slice(slot * BLK, (slot + 1) * BLK)
            rows = [kept[slot : slot + 1]]
            rows += list(high_low(turned[h : h + 1, lanes]))
            rows += list(high_low(turned[H + h : H + h + 1, lanes]))
            rows.append(jnp.zeros((3, 128), F32))
            qb_out[seat(h, slot), BLK:] = jnp.concatenate(rows, axis=0).astype(BF)


def attend_kernel(
    coef, keep, own, before, after, qb, mq_out, mqt_out, own_out, before_out, after_out,
    kvall, kvt, acc, wbuf, sems,
):
    copies = []
    for number, src in enumerate((before, own, after)):
        copies.append(pltpu.make_async_copy(src, kvall.at[:, number], sems.at[number]))
    for copy in copies:
        copy.start()
    acc[...] = jnp.zeros_like(acc)
    for copy in copies:
        copy.wait()
    for place in range(16):
        for t in range(3):
            kvt[place, :, t * BLK : (t + 1) * BLK] = kvall[place, t].T

    exp_coef = coef[0]
    grad_coef = coef[1]
    lane = lax.broadcasted_iota(jnp.int32, (BLK, 2 * DH), 1)
    low = (lane < DH).astype(F32).astype(BF)
    high = (lane >= DH).astype(F32).astype(BF)

    def fold(values):
        return jnp.sum(values.reshape(-1, 8, BLK), axis=0)

    def one_block(number, carry):
        x = number // 4
        y = number % 4
        both = qb[number, :BLK, :]
        spread = jnp.concatenate([both * low, both * high], axis=0)
        total = jnp.zeros((8, BLK), F32)
        inner = jnp.zeros((8, BLK), F32)
        for g in range(9):
            dx, dy = g // 3, g % 3
            place = (x + dx + 3) % 4 * 4 + (y + dy + 3) % 4
            keys = kvall[place].reshape(3 * BLK, 2 * DH)
            pair = dot_nt(keys, spread)
            for k in range(3):
                score = pair[k * BLK : (k + 1) * BLK, :BLK]
                slope = pair[k * BLK : (k + 1) * BLK, BLK:]
                weight = jnp.exp2(score * exp_coef) * keep[number * NB + g * 3 + k]
                total = total + fold(weight)
                inner = inner + fold(weight * slope)
                base = (g * 3 + k) * BLK
                wbuf[base : base + BLK, :BLK] = weight
                wbuf[base : base + BLK, BLK:] = slope
        total_row = jnp.sum(total, axis=0, keepdims=True)
        inverse = 1.0 / total_row
        inner_row = jnp.sum(inner, axis=0, keepdims=True) * inverse
        out = jnp.zeros((2 * DH, 2 * BLK), F32)
        for g in range(9):
            dx, dy = g // 3, g % 3
            place = (x + dx + 3) % 4 * 4 + (y + dy + 3) % 4
            base = g * 3 * BLK
            prob = wbuf[base : base + 3 * BLK, :BLK] * inverse
            slope = wbuf[base : base + 3 * BLK, BLK:]
            scaled = (prob * (slope - inner_row)) * grad_coef
            mixed = jnp.concatenate([scaled.astype(BF), prob.astype(BF)], axis=1)
            update = dot_nn(mixed, spread)
            acc[place] += update.reshape(3, BLK, 2 * DH)
            out = out + dot_nn(kvt[place], mixed)
        extra = qb[number, BLK:, :].astype(F32)
        factor = extra[1:2] + extra[2:3]
        query_t = both.astype(F32).T[:DH]
        grad_t = out[:DH, :BLK]
        inside = jnp.sum(query_t * grad_t, axis=0, keepdims=True)
        query_d = (grad_t - query_t * (inside * (1.0 / DH))) * factor
        joined = jnp.concatenate([out[DH:, BLK:], query_d], axis=0)
        mq_out[number, :BLK, :] = joined.T.astype(BF)
        mqt_out[number] = joined.astype(BF)
        return carry + inside

    inside = lax.fori_loop(0, 16, one_block, jnp.zeros((1, BLK), F32))
    upper, lower = high_low(jnp.broadcast_to(jnp.sum(inside, axis=1, keepdims=True), (1, BLK)))
    tail = jnp.concatenate([upper, lower, jnp.zeros((6, BLK), F32)], axis=0).astype(BF)
    for chunk in range(16):
        mq_out[chunk, BLK:, :] = tail
    own_out[...] = acc[:, 1]
    before_out[...] = acc[:, 0].astype(BF)
    after_out[...] = acc[:, 2].astype(BF)


def head_kernel(
    site, own, low, high, kv, qb, mqt, mq, near, far, kv_out, parts_out, turned,
):
    core = site[0]
    for b in range(16):
        total = own[b] + low[b].astype(F32) + high[b].astype(F32)
        total_t = total.T
        key_t = kv[b].astype(F32).T[:DH]
        extra = qb[b, BLK:, :].astype(F32)
        factor = extra[3:4] + extra[4:5]
        grad_t = total_t[:DH]
        inside = jnp.sum(key_t * grad_t, axis=0, keepdims=True) * (1.0 / DH)
        joined = jnp.concatenate([(grad_t - key_t * inside) * factor, total_t[DH:]], axis=0)
        turned[b] = joined.astype(BF)
        target_x = jnp.bitwise_xor(site[1], b // 4)
        target_y = jnp.bitwise_xor(site[2], b % 4)
        kv_out[target_x, target_y] = joined.T.astype(BF)
    query_part = jnp.zeros((DH, D), F32)
    proj_part = jnp.zeros((DH, D), F32)
    both_part = jnp.zeros((2 * DH, D), F32)
    for which, source in ((core, near), (1 - core, far)):
        for half in range(2):
            rows = source[half * 4 : half * 4 + 4].reshape(4 * BLK, 2 * D)
            hidden, cot = rows[:, :D], rows[:, D:]
            spots = [(half * 4 + k) * 2 + which for k in range(4)]
            mixed_t = jnp.concatenate([mqt[spot] for spot in spots], axis=1)
            both_t = jnp.concatenate([turned[spot] for spot in spots], axis=1)
            proj_part = proj_part + dot_nn(mixed_t[:DH], cot)
            query_part = query_part + dot_nn(mixed_t[DH:], hidden)
            both_part = both_part + dot_nn(both_t, hidden)
    lines = []
    for row in (BLK, BLK + 1):
        pairs = [
            mq[seat(h, 0), row : row + 1].astype(F32) + mq[seat(h, 1), row : row + 1].astype(F32)
            for h in range(H)
        ]
        lines.append(0.5 * jnp.concatenate(pairs, axis=0))
    whole_sum = lines[0] + lines[1]
    upper, lower = high_low(whole_sum)
    extra = jnp.concatenate([upper, lower, upper, lower], axis=1).astype(BF)
    joined = jnp.concatenate([query_part, both_part, proj_part], axis=0).astype(BF)
    for g in range(16):
        parts_out[g, :16] = joined[g * 16 : (g + 1) * 16]
        parts_out[g, 16:] = extra


def sum_kernel(arrived, share_out, temper_out):
    total = jnp.zeros((24, D), F32)
    for g in range(16):
        total = total + arrived[g].astype(F32)
    temper_out[...] = total[16:, :128] + total[16:, 128:256]
    share = total[:16].astype(BF)
    for k in range(64):
        share_out[k] = share


def output_kernel(core, near, far, gain, wq, wk, wv, gq, gk, gv, gp, gg, turned):
    for which, source in ((core[0], near), (1 - core[0], far)):
        for chip in range(64):
            gx, zl, tx, zh = chip // 16, chip // 8 % 2, chip // 2 % 4, chip % 2
            quarter = tx % 2 * 2 + zh
            start = pl.multiple_of(gx * 128 + which * 64 + quarter * 16, 16)
            turned[zl * 2 + tx // 2, pl.ds(start, 16), :] = source[chip]
    gp[...] = turned[3].astype(F32)
    total = jnp.zeros((D, 1), F32)
    for m, (out, weight) in enumerate(((gq, wq), (gk, wk), (gv, wv))):
        value = turned[m].T.astype(F32)
        out[...] = value
        total = total + jnp.sum(value * weight[...].astype(F32), axis=1, keepdims=True)
    line = jnp.broadcast_to(total, (D, 128)).T
    gg[...] = line[:1] / gain[...]


def finish_kernel(
    site, tok, gain, mq, kv0, kv1, kv2, kv3, wq, wk, wv, wp, layer_out, grad_tok, kv,
):
    for step_y, piece in enumerate((kv0, kv1, kv2, kv3)):
        for step_x in range(4):
            source_x = jnp.bitwise_xor(site[1], step_x)
            source_y = jnp.bitwise_xor(site[2], step_y)
            kv[source_x * 4 + source_y] = piece[step_x]

    def gathered(ref, lanes):
        halves = [
            jnp.concatenate([ref[seat(h, slot), :BLK, lanes] for h in range(H)], axis=1)
            for slot in range(2)
        ]
        return jnp.concatenate(halves, axis=0)

    left, right = slice(0, DH), slice(DH, 2 * DH)
    unit, factor_in, _ = normed_hidden(tok[...], gain[...])
    layer_out[...] = dot_nn(gathered(mq, left), wp[...]).astype(BF)
    query_d, key_d, value_d = gathered(mq, right), gathered(kv, left), gathered(kv, right)
    back_hidden = dot_nt(query_d, wq[...]) + dot_nt(key_d, wk[...]) + dot_nt(value_d, wv[...])
    slope_in = back_hidden * gain[...]
    grad_tok[...] = factor_in * (
        slope_in - unit * jnp.mean(slope_in * unit, axis=-1, keepdims=True)
    )


def whole(shape, dtype):
    return jax.ShapeDtypeStruct(shape, dtype)


def shift(block, step):
    spots = [(t % 2) * 8 + t // 2 for t in range(16)]
    return lax.ppermute(block, RING, [(spots[t], spots[(t + step) % 16]) for t in range(16)])


def swap_cores(block):
    return lax.ppermute(block, "cr", [(0, 1), (1, 0)])


def swap_near(block, axes, step):
    return lax.ppermute(block, axes, [(i, i ^ step) for i in range(4)])


def local(
    tokens, norm_gain, w_query, w_key, w_value, w_proj, temper, neighbours, valid_mask, cotangent
):
    tok = tokens.reshape(ROWS, D)
    cot = cotangent.reshape(ROWS, D)
    gain = norm_gain.reshape(1, D)
    core = lax.axis_index("cr")
    place = jnp.stack(
        [
            lax.axis_index("gx"),
            lax.axis_index("zl") * 2 + core,
            (lax.axis_index("tx") * 2 + lax.axis_index("zh")) * 2,
        ]
    )
    any_spec = pl.BlockSpec(memory_space=pl.ANY)
    smem = pl.BlockSpec(memory_space=pltpu.SMEM)
    vmem = pl.BlockSpec(memory_space=pltpu.VMEM)

    pair = (16, BLK, 2 * DH)
    wide = (16, BLK + EXTRA, 2 * DH)
    kv_send, qb_send, rows_send = pl.pallas_call(
        project_kernel,
        cost_estimate=cost(6),
        out_shape=(whole(pair, BF), whole(wide, BF), whole((8, BLK, 2 * D), BF)),
        in_specs=[smem] + [vmem] * 9,
        out_specs=(vmem, vmem, vmem),
        compiler_params=params(),
    )(
        place, tok, gain, cot, neighbours.reshape(2, NB), valid_mask.reshape(2, NB),
        w_query, w_key, w_value, w_proj,
    )

    own = lax.all_to_all(kv_send, GROUP, 0, 0, tiled=True)
    before = shift(own, 1)
    after = shift(own, -1)
    qb_send, own = lax.optimization_barrier((qb_send, own))
    qb = lax.all_to_all(qb_send, GROUP, 0, 0, tiled=True)
    rows_send, qb, before, after = lax.optimization_barrier((rows_send, qb, before, after))
    rows_near = lax.all_to_all(rows_send, ("gx", "zl"), 0, 0, tiled=True)
    keep = qb[:, BLK, :NB].astype(F32).reshape(16 * NB)
    head_id = lax.axis_index("gx") * 2 + core
    temp = temper[head_id] * SCALE
    coef = jnp.stack([temp * math.log2(math.e), temp])

    mq_send, mqt, own_grad, before_grad, after_grad = pl.pallas_call(
        attend_kernel,
        cost_estimate=cost(36),
        out_shape=(
            whole(wide, BF), whole((16, 2 * DH, BLK), BF), whole(pair, F32),
            whole(pair, BF), whole(pair, BF),
        ),
        in_specs=[smem, smem] + [any_spec] * 3 + [vmem],
        out_specs=tuple([vmem] * 5),
        scratch_shapes=[
            pltpu.VMEM((16, 3, BLK, 2 * DH), BF),
            pltpu.VMEM((16, 2 * DH, 3 * BLK), BF),
            pltpu.VMEM((16, 3, BLK, 2 * DH), F32),
            pltpu.VMEM((NB * BLK, 2 * BLK), F32),
            pltpu.SemaphoreType.DMA((3,)),
        ],
        compiler_params=params(),
    )(coef, keep, own, before, after, qb)
    from_after = shift(before_grad, -1)
    from_before = shift(after_grad, 1)
    rows_near, mq_send = lax.optimization_barrier((rows_near, mq_send))
    rows_far = swap_cores(rows_near)
    mq = lax.all_to_all(mq_send, GROUP, 0, 0, tiled=True)
    site = jnp.stack([core, lax.axis_index("gx"), lax.axis_index("zl") * 2 + core])
    kv_back, parts = pl.pallas_call(
        head_kernel,
        cost_estimate=cost(7),
        out_shape=(whole((4, 4, BLK, 2 * DH), BF), whole((16, 24, D), BF)),
        in_specs=[smem] + [vmem] * 9,
        scratch_shapes=[pltpu.VMEM((16, 2 * DH, BLK), BF)],
        compiler_params=params(),
    )(site, own_grad, from_after, from_before, own, qb, mqt, mq, rows_near, rows_far)
    arrived = lax.all_to_all(parts, RING, 0, 0, tiled=True)
    turn = [kv_back[0]] + [swap_near(kv_back[step], "gx", step) for step in range(1, 4)]
    arrived, *turn = lax.optimization_barrier((arrived, *turn))
    share, temper_sum = pl.pallas_call(
        sum_kernel,
        cost_estimate=cost(2),
        out_shape=(whole((64, 16, D), BF), whole((H, 128), F32)),
        compiler_params=params(),
    )(arrived)
    near = lax.all_to_all(share, CHIPS, 0, 0, tiled=True)
    kv = [jnp.stack([piece[step] for piece in turn]) for step in range(4)]
    kv = [kv[0]] + [swap_near(kv[step], ("zl", "cr"), step) for step in range(1, 4)]
    near, *kv = lax.optimization_barrier((near, *kv))
    layer_out, grad_tokens = pl.pallas_call(
        finish_kernel,
        cost_estimate=cost(4),
        out_shape=(whole((ROWS, D), BF), whole((ROWS, D), F32)),
        in_specs=[smem] + [vmem] * 11,
        scratch_shapes=[pltpu.VMEM(pair, BF)],
        compiler_params=params(),
    )(site, tok, gain, mq, *kv, w_query, w_key, w_value, w_proj)
    far = swap_cores(near)
    square = whole((D, D), F32)
    gq, gk, gv, gp, grad_gain = pl.pallas_call(
        output_kernel,
        cost_estimate=cost(5),
        out_shape=(square, square, square, square, whole((1, D), F32)),
        in_specs=[smem] + [vmem] * 6,
        scratch_shapes=[pltpu.VMEM((4, D, D), BF)],
        compiler_params=params(),
    )(core.reshape(1), near, far, gain, w_query, w_key, w_value)
    grad_temper = temper_sum[:, 0] / temper
    return (
        layer_out.reshape(tokens.shape),
        grad_tokens.reshape(tokens.shape),
        grad_gain.reshape(D),
        gq,
        gk,
        gv,
        gp,
        grad_temper,
    )


def solution(mesh):
    fine = Mesh(mesh.devices.reshape(4, 2, 2, 4, 2), ALL)
    lattice = ("gx", ("zl", "cr"), ("tx", "zh"))
    blocks = P(*lattice, None, None)
    lists = P(*lattice, None)
    return jax.shard_map(
        local,
        mesh=fine,
        in_specs=(blocks, P(), P(), P(), P(), P(), P(), lists, lists, blocks),
        out_specs=(blocks, blocks, P(), P(), P(), P(), P(), P()),
        check_vma=False,
    )
```

```python
import math

import jax
import jax.numpy as jnp
from jax import lax
from jax.experimental import pallas as pl
from jax.experimental.pallas import tpu as pltpu
from jax.sharding import Mesh, PartitionSpec as P

NORM_EPS = 1e-05
HEAD_EPS = 1e-06
D = 512
H = 8
DH = 64
BLK = 128
NB = 27
ROWS = 256
SCALE = DH**-0.5
BF = jnp.bfloat16
F32 = jnp.float32
GROUP = ("gx", "zl", "cr")
RING = ("zl", "tx", "zh")
CHIPS = ("gx", "zl", "tx", "zh")
ALL = ("gx", "zl", "cr", "tx", "zh")
EXTRA = 8
VMEM_LIMIT = 56 * 1024 * 1024


def params():
    return pltpu.CompilerParams(vmem_limit_bytes=VMEM_LIMIT)


def cost(micros):
    return pl.CostEstimate(
        flops=int(micros * 1e9), bytes_accessed=int(micros * 1e6), transcendentals=0
    )


def dot_nn(left, right):
    return jnp.dot(left, right, preferred_element_type=F32)


def dot_nt(left, right):
    return lax.dot_general(left, right, (((1,), (1,)), ((), ())), preferred_element_type=F32)


def dot_tn(left, right):
    return lax.dot_general(left, right, (((0,), (0,)), ((), ())), preferred_element_type=F32)


def head(values, index):
    return values[:, index * DH : (index + 1) * DH]


def normed_hidden(tokens, gain):
    values = tokens.astype(F32)
    factor = lax.rsqrt(jnp.mean(values * values, axis=-1, keepdims=True) + NORM_EPS)
    unit = values * factor
    return unit, factor, (unit * gain).astype(BF)


def high_low(values):
    upper = values.astype(BF).astype(F32)
    return upper, values - upper


def seat(h, slot):
    return (h // 2) * 4 + slot * 2 + h % 2


def key_kernel(tok, gain, wk, wv, kv_out, fac_out):
    _, _, hidden = normed_hidden(tok[...], gain[...])
    lane = lax.broadcasted_iota(jnp.int32, (ROWS, 128), 1)
    factors = jnp.zeros((ROWS, 128), F32)
    key_f = dot_nn(hidden, wk[...])
    value = dot_nn(hidden, wv[...]).astype(BF)
    for h in range(H):
        part = head(key_f, h)
        factor = lax.rsqrt(jnp.mean(part * part, axis=-1, keepdims=True) + HEAD_EPS)
        factors = jnp.where(lane == H + h, factor, factors)
        joined = jnp.concatenate([(part * factor).astype(BF), head(value, h)], axis=1)
        kv_out[seat(h, 0)] = joined[:BLK]
        kv_out[seat(h, 1)] = joined[BLK:]
    fac_out[...] = factors


def query_kernel(tok, gain, cot, neighbours, valid, factors_in, wq, wp, qb_out, rows_out):
    _, _, hidden = normed_hidden(tok[...], gain[...])
    for k in range(8):
        lines = slice((k % 2) * BLK, (k % 2 + 1) * BLK)
        rows_out[k, :, :D] = hidden[lines]
        rows_out[k, :, D:] = cot[lines]
    lane = lax.broadcasted_iota(jnp.int32, (ROWS, 128), 1)
    factors = factors_in[...]
    query_f = dot_nn(hidden, wq[...])
    back = dot_nt(cot[...], wp[...]).astype(BF)
    for h in range(H):
        part = head(query_f, h)
        factor = lax.rsqrt(jnp.mean(part * part, axis=-1, keepdims=True) + HEAD_EPS)
        factors = jnp.where(lane == h, factor, factors)
        joined = jnp.concatenate([(part * factor).astype(BF), head(back, h)], axis=1)
        qb_out[seat(h, 0), :BLK] = joined[:BLK]
        qb_out[seat(h, 1), :BLK] = joined[BLK:]
    ids = neighbours[...]
    keep = valid[...]
    place_y = lax.axis_index("zl") * 2 + lax.axis_index("cr")
    place_t = (lax.axis_index("tx") * 2 + lax.axis_index("zh")) * 2
    own_t = place_t + lax.broadcasted_iota(jnp.int32, (2, NB), 0)
    step_t = jnp.bitwise_and(ids - own_t + 1, 15)
    step_y = jnp.bitwise_and(jnp.right_shift(ids, 4) - place_y + 1, 3)
    step_x = jnp.bitwise_and(jnp.right_shift(ids, 6) - lax.axis_index("gx") + 1, 3)
    slots = step_x * 9 + step_y * 3 + step_t
    short = lax.broadcasted_iota(jnp.int32, (2, 128), 1)
    kept = jnp.zeros((2, 128), F32)
    for slot in range(NB):
        hit = short == slots[:, slot : slot + 1]
        kept = kept + jnp.where(hit, keep[:, slot : slot + 1].astype(F32), 0.0)
    turned = factors.T
    for h in range(H):
        for slot in range(2):
            lanes = slice(slot * BLK, (slot + 1) * BLK)
            rows = [kept[slot : slot + 1]]
            rows += list(high_low(turned[h : h + 1, lanes]))
            rows += list(high_low(turned[H + h : H + h + 1, lanes]))
            rows.append(jnp.zeros((3, 128), F32))
            qb_out[seat(h, slot), BLK:] = jnp.concatenate(rows, axis=0).astype(BF)


def attend_kernel(
    coef, own, before, after, qb, mq_out, mqt_out, own_out, before_out, after_out,
    kvall, kvt, acc, wbuf, wbuf2, keep_rows, keep, sems,
):
    copies = []
    for number, src in enumerate((before, own, after)):
        copies.append(pltpu.make_async_copy(src, kvall.at[:, number], sems.at[number]))
    for copy in copies:
        copy.start()
    for number in range(16):
        keep_rows[number : number + 1] = qb[number, BLK:, :].astype(F32)[:1]
    copies.append(pltpu.make_async_copy(keep_rows, keep, sems.at[3]))
    copies[3].start()
    acc[...] = jnp.zeros_like(acc)
    for copy in copies:
        copy.wait()
    for place in range(16):
        for t in range(3):
            kvt[place, :, t * BLK : (t + 1) * BLK] = kvall[place, t].T

    exp_coef = coef[0]
    grad_coef = coef[1]
    lane = lax.broadcasted_iota(jnp.int32, (BLK, 2 * DH), 1)
    low = (lane < DH).astype(F32).astype(BF)
    high = (lane >= DH).astype(F32).astype(BF)

    def fold(values):
        return jnp.sum(values.reshape(-1, 8, BLK), axis=0)

    def spread_of(number):
        both = qb[number, :BLK, :]
        return jnp.concatenate([both * low, both * high], axis=0)

    def place_of(number, g):
        return (number // 4 + g // 3 + 3) % 4 * 4 + (number % 4 + g % 3 + 3) % 4

    def first_group(number, g, spread, sums, buffer):
        keys = kvall[place_of(number, g)].reshape(3 * BLK, 2 * DH)
        pair = dot_nt(keys, spread)
        total, inner = sums
        for k in range(3):
            score = pair[k * BLK : (k + 1) * BLK, :BLK] * exp_coef
            slope = pair[k * BLK : (k + 1) * BLK, BLK:]
            weight = jnp.exp2(score)
            slot = g * 3 + k
            kept = keep[number, slot]
            total = total + fold(weight) * kept
            inner = inner + fold(weight * slope) * kept
            base = (g * 3 + k) * BLK
            buffer[base : base + BLK, :BLK] = score
            buffer[base : base + BLK, BLK:] = slope
        return total, inner

    def second_group(number, g, spread, inverse, inner_row, out, heat, buffer):
        place = place_of(number, g)
        pieces = []
        for k in range(3):
            slot = g * 3 + k
            base = slot * BLK
            score = buffer[base : base + BLK, :BLK]
            prob = jnp.exp2(score) * (inverse * keep[number, slot])
            slope = buffer[base : base + BLK, BLK:]
            grad = prob * (slope - inner_row)
            heat = heat + fold(grad * score)
            scaled = grad * grad_coef
            pieces.append(jnp.concatenate([scaled.astype(BF), prob.astype(BF)], axis=1))
        mixed = jnp.concatenate(pieces, axis=0)
        acc[place] += dot_nn(mixed, spread).reshape(3, BLK, 2 * DH)
        return out + dot_nn(kvt[place], mixed), heat

    def close(number, out):
        extra = qb[number, BLK:, :].astype(F32)
        factor = extra[1:2] + extra[2:3]
        query_t = qb[number, :BLK, :].astype(F32).T[:DH]
        grad_t = out[:DH, :BLK]
        inside = jnp.sum(query_t * grad_t, axis=0, keepdims=True)
        query_d = (grad_t - query_t * (inside * (1.0 / DH))) * factor
        joined = jnp.concatenate([out[DH:, BLK:], query_d], axis=0)
        mq_out[number, :BLK, :] = joined.T.astype(BF)
        mqt_out[number] = joined.astype(BF)

    zero = jnp.zeros((8, BLK), F32)

    def step(number, following, sums, heat, buffer, other):
        inverse = 1.0 / jnp.sum(sums[0], axis=0, keepdims=True)
        inner_row = jnp.sum(sums[1], axis=0, keepdims=True) * inverse
        spread = spread_of(number)
        next_spread = spread_of(following)
        next_sums = (zero, zero)
        out = jnp.zeros((2 * DH, 2 * BLK), F32)
        for g in range(9):
            next_sums = first_group(following, g, next_spread, next_sums, other)
            out, heat = second_group(
                number, g, spread, inverse, inner_row, out, heat, buffer
            )
        close(number, out)
        return next_sums, heat

    sums = (zero, zero)
    first_spread = spread_of(0)
    for g in range(9):
        sums = first_group(0, g, first_spread, sums, wbuf)

    def two_blocks(index, carry):
        sums, heat = carry
        number = index * 2
        sums, heat = step(number, number + 1, sums, heat, wbuf, wbuf2)
        following = jnp.minimum(number + 2, 15)
        return step(number + 1, following, sums, heat, wbuf2, wbuf)

    _, heat = lax.fori_loop(0, 8, two_blocks, (sums, zero))
    heat = jnp.sum(jnp.sum(heat, axis=0, keepdims=True), axis=1, keepdims=True)
    upper, lower = high_low(jnp.broadcast_to(heat, (1, BLK)))
    tail = jnp.concatenate([upper, lower, jnp.zeros((6, BLK), F32)], axis=0).astype(BF)
    for chunk in range(16):
        mq_out[chunk, BLK:, :] = tail
    own_out[...] = acc[:, 1]
    before_out[...] = acc[:, 0].astype(BF)
    after_out[...] = acc[:, 2].astype(BF)


def early_kernel(site, mqt, near, far, out):
    query_part = jnp.zeros((DH, D), F32)
    proj_part = jnp.zeros((DH, D), F32)
    for which, source in ((site[0], near), (1 - site[0], far)):
        for half in range(2):
            rows = source[half * 4 : half * 4 + 4].reshape(4 * BLK, 2 * D)
            spots = [(half * 4 + k) * 2 + which for k in range(4)]
            mixed_t = jnp.concatenate([mqt[spot] for spot in spots], axis=1)
            proj_part = proj_part + dot_nn(mixed_t[:DH], rows[:, D:])
            query_part = query_part + dot_nn(mixed_t[DH:], rows[:, :D])
    out[...] = jnp.concatenate([query_part, proj_part], axis=0).astype(BF)


def head_kernel(
    site, own, low, high, kv, qb, early, mq, near, far, kv_out, parts_out, turned,
):
    core = site[0]
    for b in range(16):
        total = own[b] + low[b].astype(F32) + high[b].astype(F32)
        total_t = total.T
        key_t = kv[b].astype(F32).T[:DH]
        extra = qb[b, BLK:, :].astype(F32)
        factor = extra[3:4] + extra[4:5]
        grad_t = total_t[:DH]
        inside = jnp.sum(key_t * grad_t, axis=0, keepdims=True) * (1.0 / DH)
        joined = jnp.concatenate([(grad_t - key_t * inside) * factor, total_t[DH:]], axis=0)
        turned[b] = joined.astype(BF)
        target_x = jnp.bitwise_xor(site[1], b // 4)
        target_y = jnp.bitwise_xor(site[2], b % 4)
        kv_out[target_x, target_y] = joined.T.astype(BF)
    both_part = jnp.zeros((2 * DH, D), F32)
    for which, source in ((core, near), (1 - core, far)):
        for half in range(2):
            hidden = source[half * 4 : half * 4 + 4].reshape(4 * BLK, D)
            spots = [(half * 4 + k) * 2 + which for k in range(4)]
            both_t = jnp.concatenate([turned[spot] for spot in spots], axis=1)
            both_part = both_part + dot_nn(both_t, hidden)
    lines = []
    for row in (BLK, BLK + 1):
        pairs = [
            mq[seat(h, 0), row : row + 1].astype(F32) + mq[seat(h, 1), row : row + 1].astype(F32)
            for h in range(H)
        ]
        lines.append(0.5 * jnp.concatenate(pairs, axis=0))
    whole_sum = lines[0] + lines[1]
    upper, lower = high_low(whole_sum)
    extra = jnp.concatenate([upper, lower, upper, lower], axis=1).astype(BF)
    query_part, proj_part = early[:DH], early[DH:]
    joined = jnp.concatenate([query_part, both_part.astype(BF), proj_part], axis=0)
    for g in range(16):
        parts_out[g, :16] = joined[g * 16 : (g + 1) * 16]
        parts_out[g, 16:] = extra


def sum_kernel(arrived, share_out, temper_out):
    total = jnp.zeros((24, D), F32)
    for g in range(16):
        total = total + arrived[g].astype(F32)
    temper_out[...] = total[16:, :128] + total[16:, 128:256]
    share = total[:16].astype(BF)
    for k in range(64):
        share_out[k] = share


def output_kernel(core, near, far, gain, wq, wk, wv, gq, gk, gv, gp, gg, turned):
    for which, source in ((core[0], near), (1 - core[0], far)):
        for chip in range(64):
            gx, zl, tx, zh = chip // 16, chip // 8 % 2, chip // 2 % 4, chip % 2
            quarter = tx % 2 * 2 + zh
            start = pl.multiple_of(gx * 128 + which * 64 + quarter * 16, 16)
            turned[zl * 2 + tx // 2, pl.ds(start, 16), :] = source[chip]
    gp[...] = turned[3].astype(F32)
    total = jnp.zeros((D, 1), F32)
    for m, (out, weight) in enumerate(((gq, wq), (gk, wk), (gv, wv))):
        value = turned[m].T.astype(F32)
        out[...] = value
        total = total + jnp.sum(value * weight[...].astype(F32), axis=1, keepdims=True)
    line = jnp.broadcast_to(total, (D, 128)).T
    gg[...] = line[:1] / gain[...]


def finish_kernel(
    site, tok, gain, mq, kv0, kv1, kv2, kv3, wq, wk, wv, wp, layer_out, grad_tok, kv,
):
    for step_y, piece in enumerate((kv0, kv1, kv2, kv3)):
        for step_x in range(4):
            source_x = jnp.bitwise_xor(site[1], step_x)
            source_y = jnp.bitwise_xor(site[2], step_y)
            kv[source_x * 4 + source_y] = piece[step_x]

    def gathered(ref, lanes):
        halves = [
            jnp.concatenate([ref[seat(h, slot), :BLK, lanes] for h in range(H)], axis=1)
            for slot in range(2)
        ]
        return jnp.concatenate(halves, axis=0)

    left, right = slice(0, DH), slice(DH, 2 * DH)
    unit, factor_in, _ = normed_hidden(tok[...], gain[...])
    layer_out[...] = dot_nn(gathered(mq, left), wp[...]).astype(BF)
    query_d, key_d, value_d = gathered(mq, right), gathered(kv, left), gathered(kv, right)
    back_hidden = dot_nt(query_d, wq[...]) + dot_nt(key_d, wk[...]) + dot_nt(value_d, wv[...])
    slope_in = back_hidden * gain[...]
    grad_tok[...] = factor_in * (
        slope_in - unit * jnp.mean(slope_in * unit, axis=-1, keepdims=True)
    )


def whole(shape, dtype):
    return jax.ShapeDtypeStruct(shape, dtype)


def shift(block, step):
    spots = [(t % 2) * 8 + t // 2 for t in range(16)]
    return lax.ppermute(block, RING, [(spots[t], spots[(t + step) % 16]) for t in range(16)])


def swap_cores(block):
    return lax.ppermute(block, "cr", [(0, 1), (1, 0)])


def swap_near(block, axes, step):
    return lax.ppermute(block, axes, [(i, i ^ step) for i in range(4)])


def local(
    tokens, norm_gain, w_query, w_key, w_value, w_proj, temper, neighbours, valid_mask, cotangent
):
    tok = tokens.reshape(ROWS, D)
    cot = cotangent.reshape(ROWS, D)
    gain = norm_gain.reshape(1, D)
    core = lax.axis_index("cr")
    any_spec = pl.BlockSpec(memory_space=pl.ANY)
    smem = pl.BlockSpec(memory_space=pltpu.SMEM)
    vmem = pl.BlockSpec(memory_space=pltpu.VMEM)

    pair = (16, BLK, 2 * DH)
    wide = (16, BLK + EXTRA, 2 * DH)
    kv_send, factors = pl.pallas_call(
        key_kernel,
        cost_estimate=cost(3),
        out_shape=(whole(pair, BF), whole((ROWS, 128), F32)),
        compiler_params=params(),
    )(tok, gain, w_key, w_value)
    qb_send, rows_send = pl.pallas_call(
        query_kernel,
        cost_estimate=cost(4),
        out_shape=(whole(wide, BF), whole((8, BLK, 2 * D), BF)),
        compiler_params=params(),
    )(
        tok, gain, cot, neighbours.reshape(2, NB), valid_mask.reshape(2, NB), factors,
        w_query, w_proj,
    )

    own = lax.all_to_all(kv_send, GROUP, 0, 0, tiled=True)
    qb_send, own = lax.optimization_barrier((qb_send, own))
    before = shift(own, 1)
    after = shift(own, -1)
    qb = lax.all_to_all(qb_send, GROUP, 0, 0, tiled=True)
    rows_send, qb, before, after = lax.optimization_barrier((rows_send, qb, before, after))
    rows_near = lax.all_to_all(rows_send, ("gx", "zl"), 0, 0, tiled=True)
    head_id = lax.axis_index("gx") * 2 + core
    temp = temper[head_id] * SCALE
    coef = jnp.stack([temp * math.log2(math.e), temp])

    mq_send, mqt, own_grad, before_grad, after_grad = pl.pallas_call(
        attend_kernel,
        cost_estimate=cost(36),
        out_shape=(
            whole(wide, BF), whole((16, 2 * DH, BLK), BF), whole(pair, F32),
            whole(pair, BF), whole(pair, BF),
        ),
        in_specs=[smem] + [any_spec] * 3 + [vmem],
        out_specs=tuple([vmem] * 5),
        scratch_shapes=[
            pltpu.VMEM((16, 3, BLK, 2 * DH), BF),
            pltpu.VMEM((16, 2 * DH, 3 * BLK), BF),
            pltpu.VMEM((16, 3, BLK, 2 * DH), F32),
            pltpu.VMEM((NB * BLK, 2 * BLK), F32),
            pltpu.VMEM((NB * BLK, 2 * BLK), F32),
            pltpu.VMEM((16, 128), F32),
            pltpu.SMEM((16, 128), F32),
            pltpu.SemaphoreType.DMA((4,)),
        ],
        compiler_params=params(),
    )(coef, own, before, after, qb)
    from_after = shift(before_grad, -1)
    from_before = shift(after_grad, 1)
    rows_near, mq_send = lax.optimization_barrier((rows_near, mq_send))
    rows_far = swap_cores(rows_near)
    mq = lax.all_to_all(mq_send, GROUP, 0, 0, tiled=True)
    site = jnp.stack([core, lax.axis_index("gx"), lax.axis_index("zl") * 2 + core])
    early = pl.pallas_call(
        early_kernel,
        cost_estimate=cost(3),
        out_shape=whole((2 * DH, D), BF),
        in_specs=[smem] + [vmem] * 3,
        compiler_params=params(),
    )(site, mqt, rows_near, rows_far)
    hidden_spec = pl.BlockSpec((8, BLK, D), lambda i: (0, 0, 0))

    def one_spec(array):
        return pl.BlockSpec(array.shape, lambda i: (0,) * array.ndim)

    kv_back, parts = pl.pallas_call(
        head_kernel,
        cost_estimate=cost(7),
        out_shape=(whole((4, 4, BLK, 2 * DH), BF), whole((16, 24, D), BF)),
        grid=(1,),
        in_specs=[smem]
        + [one_spec(a) for a in (own_grad, from_after, from_before, own, qb, early, mq)]
        + [hidden_spec, hidden_spec],
        scratch_shapes=[pltpu.VMEM((16, 2 * DH, BLK), BF)],
        compiler_params=params(),
    )(site, own_grad, from_after, from_before, own, qb, early, mq, rows_near, rows_far)
    arrived = lax.all_to_all(parts, RING, 0, 0, tiled=True)
    turn = [kv_back[0]] + [swap_near(kv_back[step], "gx", step) for step in range(1, 4)]
    arrived, *turn = lax.optimization_barrier((arrived, *turn))
    share, temper_sum = pl.pallas_call(
        sum_kernel,
        cost_estimate=cost(2),
        out_shape=(whole((64, 16, D), BF), whole((H, 128), F32)),
        compiler_params=params(),
    )(arrived)
    near = lax.all_to_all(share, CHIPS, 0, 0, tiled=True)
    kv = [jnp.stack([piece[step] for piece in turn]) for step in range(4)]
    kv = [kv[0]] + [swap_near(kv[step], ("zl", "cr"), step) for step in range(1, 4)]
    near, *kv = lax.optimization_barrier((near, *kv))
    layer_out, grad_tokens = pl.pallas_call(
        finish_kernel,
        cost_estimate=cost(4),
        out_shape=(whole((ROWS, D), BF), whole((ROWS, D), F32)),
        in_specs=[smem] + [vmem] * 11,
        scratch_shapes=[pltpu.VMEM(pair, BF)],
        compiler_params=params(),
    )(site, tok, gain, mq, *kv, w_query, w_key, w_value, w_proj)
    far = swap_cores(near)
    square = whole((D, D), F32)
    gq, gk, gv, gp, grad_gain = pl.pallas_call(
        output_kernel,
        cost_estimate=cost(5),
        out_shape=(square, square, square, square, whole((1, D), F32)),
        in_specs=[smem] + [vmem] * 6,
        scratch_shapes=[pltpu.VMEM((4, D, D), BF)],
        compiler_params=params(),
    )(core.reshape(1), near, far, gain, w_query, w_key, w_value)
    grad_temper = temper_sum[:, 0] / (temper * math.log2(math.e))
    return (
        layer_out.reshape(tokens.shape),
        grad_tokens.reshape(tokens.shape),
        grad_gain.reshape(D),
        gq,
        gk,
        gv,
        gp,
        grad_temper,
    )


def solution(mesh):
    fine = Mesh(mesh.devices.reshape(4, 2, 2, 4, 2), ALL)
    lattice = ("gx", ("zl", "cr"), ("tx", "zh"))
    blocks = P(*lattice, None, None)
    lists = P(*lattice, None)
    return jax.shard_map(
        local,
        mesh=fine,
        in_specs=(blocks, P(), P(), P(), P(), P(), P(), lists, lists, blocks),
        out_specs=(blocks, blocks, P(), P(), P(), P(), P(), P()),
        check_vma=False,
    )
```

```python
import math

import jax
import jax.numpy as jnp
from jax import lax
from jax.experimental import pallas as pl
from jax.experimental.pallas import tpu as pltpu
from jax.sharding import Mesh, PartitionSpec as P

NORM_EPS = 1e-05
HEAD_EPS = 1e-06
D = 512
H = 8
DH = 64
BLK = 128
NB = 27
ROWS = 256
SCALE = DH**-0.5
BF = jnp.bfloat16
F32 = jnp.float32
GROUP = ("gx", "zl", "cr")
RING = ("zl", "tx", "zh")
CHIPS = ("gx", "zl", "tx", "zh")
ALL = ("gx", "zl", "cr", "tx", "zh")
EXTRA = 8
MIB = 1024 * 1024


def params(mebibytes):
    return pltpu.CompilerParams(vmem_limit_bytes=mebibytes * MIB)


def cost(micros):
    return pl.CostEstimate(
        flops=int(micros * 1e9), bytes_accessed=int(micros * 1e6), transcendentals=0
    )


def dot_nn(left, right):
    return jnp.dot(left, right, preferred_element_type=F32)


def dot_nt(left, right):
    return lax.dot_general(left, right, (((1,), (1,)), ((), ())), preferred_element_type=F32)


def dot_tn(left, right):
    return lax.dot_general(left, right, (((0,), (0,)), ((), ())), preferred_element_type=F32)


def head(values, index):
    return values[:, index * DH : (index + 1) * DH]


def normed_hidden(tokens, gain):
    values = tokens.astype(F32)
    factor = lax.rsqrt(jnp.mean(values * values, axis=-1, keepdims=True) + NORM_EPS)
    unit = values * factor
    return unit, factor, (unit * gain).astype(BF)


def high_low(values):
    upper = values.astype(BF).astype(F32)
    return upper, values - upper


def seat(h, slot):
    return (h // 2) * 4 + slot * 2 + h % 2


def key_kernel(tok, gain, wk, wv, kv_out, fac_out):
    _, _, hidden = normed_hidden(tok[...], gain[...])
    lane = lax.broadcasted_iota(jnp.int32, (ROWS, 128), 1)
    factors = jnp.zeros((ROWS, 128), F32)
    key_f = dot_nn(hidden, wk[...])
    value = dot_nn(hidden, wv[...]).astype(BF)
    for h in range(H):
        part = head(key_f, h)
        factor = lax.rsqrt(jnp.mean(part * part, axis=-1, keepdims=True) + HEAD_EPS)
        factors = jnp.where(lane == H + h, factor, factors)
        joined = jnp.concatenate([(part * factor).astype(BF), head(value, h)], axis=1)
        kv_out[seat(h, 0)] = joined[:BLK]
        kv_out[seat(h, 1)] = joined[BLK:]
    fac_out[...] = factors


def query_kernel(tok, gain, cot, neighbours, valid, factors_in, wq, wp, qb_out, rows_out):
    _, _, hidden = normed_hidden(tok[...], gain[...])
    for k in range(8):
        lines = slice((k % 2) * BLK, (k % 2 + 1) * BLK)
        rows_out[k, :, :D] = hidden[lines]
        rows_out[k, :, D:] = cot[lines]
    lane = lax.broadcasted_iota(jnp.int32, (ROWS, 128), 1)
    factors = factors_in[...]
    query_f = dot_nn(hidden, wq[...])
    back = dot_nt(cot[...], wp[...]).astype(BF)
    for h in range(H):
        part = head(query_f, h)
        factor = lax.rsqrt(jnp.mean(part * part, axis=-1, keepdims=True) + HEAD_EPS)
        factors = jnp.where(lane == h, factor, factors)
        joined = jnp.concatenate([(part * factor).astype(BF), head(back, h)], axis=1)
        qb_out[seat(h, 0), :BLK] = joined[:BLK]
        qb_out[seat(h, 1), :BLK] = joined[BLK:]
    ids = neighbours[...]
    keep = valid[...]
    place_y = lax.axis_index("zl") * 2 + lax.axis_index("cr")
    place_t = (lax.axis_index("tx") * 2 + lax.axis_index("zh")) * 2
    own_t = place_t + lax.broadcasted_iota(jnp.int32, (2, NB), 0)
    step_t = jnp.bitwise_and(ids - own_t + 1, 15)
    step_y = jnp.bitwise_and(jnp.right_shift(ids, 4) - place_y + 1, 3)
    step_x = jnp.bitwise_and(jnp.right_shift(ids, 6) - lax.axis_index("gx") + 1, 3)
    slots = step_x * 9 + step_y * 3 + step_t
    short = lax.broadcasted_iota(jnp.int32, (2, 128), 1)
    kept = jnp.zeros((2, 128), F32)
    for slot in range(NB):
        hit = short == slots[:, slot : slot + 1]
        kept = kept + jnp.where(hit, keep[:, slot : slot + 1].astype(F32), 0.0)
    turned = factors.T
    for h in range(H):
        for slot in range(2):
            lanes = slice(slot * BLK, (slot + 1) * BLK)
            rows = [kept[slot : slot + 1]]
            rows += list(high_low(turned[h : h + 1, lanes]))
            rows += list(high_low(turned[H + h : H + h + 1, lanes]))
            rows.append(jnp.zeros((3, 128), F32))
            qb_out[seat(h, slot), BLK:] = jnp.concatenate(rows, axis=0).astype(BF)


def attend_kernel(
    coef, own, before, after, qb, mq_hbm, mqt_hbm, own_hbm, before_hbm, after_hbm,
    mq_out, mqt_out, before_out, after_out, kvall, kvt, acc, wbuf, wbuf2, keep_rows, keep, sems,
):
    copies = []
    for number, src in enumerate((before, own, after)):
        copies.append(pltpu.make_async_copy(src, kvall.at[:, number], sems.at[number]))
    for copy in copies:
        copy.start()
    for number in range(16):
        keep_rows[number : number + 1] = qb[number, BLK:, :].astype(F32)[:1]
    copies.append(pltpu.make_async_copy(keep_rows, keep, sems.at[3]))
    copies[3].start()
    acc[...] = jnp.zeros_like(acc)
    for copy in copies:
        copy.wait()
    for place in range(16):
        for t in range(3):
            kvt[place, :, t * BLK : (t + 1) * BLK] = kvall[place, t].T

    exp_coef = coef[0]
    grad_coef = coef[1]
    lane = lax.broadcasted_iota(jnp.int32, (BLK, 2 * DH), 1)
    low = (lane < DH).astype(F32).astype(BF)
    high = (lane >= DH).astype(F32).astype(BF)

    def fold(values):
        return jnp.sum(values.reshape(-1, 8, BLK), axis=0)

    def spread_of(number):
        both = qb[number, :BLK, :]
        return jnp.concatenate([both * low, both * high], axis=0)

    def place_of(number, g):
        return (number // 4 + g // 3 + 3) % 4 * 4 + (number % 4 + g % 3 + 3) % 4

    def first_group(number, g, spread, sums, buffer):
        keys = kvall[place_of(number, g)].reshape(3 * BLK, 2 * DH)
        pair = dot_nt(keys, spread)
        total, inner = sums
        for k in range(3):
            score = pair[k * BLK : (k + 1) * BLK, :BLK] * exp_coef
            slope = pair[k * BLK : (k + 1) * BLK, BLK:]
            weight = jnp.exp2(score)
            slot = g * 3 + k
            kept = keep[number, slot]
            total = total + fold(weight) * kept
            inner = inner + fold(weight * slope) * kept
            base = (g * 3 + k) * BLK
            buffer[base : base + BLK, :BLK] = score
            buffer[base : base + BLK, BLK:] = slope
        return total, inner

    def second_group(number, g, spread, inverse, inner_row, heat, buffer):
        place = place_of(number, g)
        pieces = []
        for k in range(3):
            slot = g * 3 + k
            base = slot * BLK
            score = buffer[base : base + BLK, :BLK]
            prob = jnp.exp2(score) * (inverse * keep[number, slot])
            slope = buffer[base : base + BLK, BLK:]
            grad = prob * (slope - inner_row)
            heat = heat + fold(grad * score)
            scaled = grad * grad_coef
            pieces.append(jnp.concatenate([scaled.astype(BF), prob.astype(BF)], axis=1))
        mixed = jnp.concatenate(pieces, axis=0)
        acc[place] += dot_nn(mixed, spread).reshape(3, BLK, 2 * DH)
        return kvt[place], mixed, heat

    def close(number, out):
        extra = qb[number, BLK:, :].astype(F32)
        factor = extra[1:2] + extra[2:3]
        query_t = qb[number, :BLK, :].astype(F32).T[:DH]
        grad_t = out[:DH, :BLK]
        inside = jnp.sum(query_t * grad_t, axis=0, keepdims=True)
        query_d = (grad_t - query_t * (inside * (1.0 / DH))) * factor
        joined = jnp.concatenate([out[DH:, BLK:], query_d], axis=0)
        mq_out[number, :BLK, :] = joined.T.astype(BF)
        mqt_out[number] = joined.astype(BF)

    zero = jnp.zeros((8, BLK), F32)

    def step(number, following, sums, heat, buffer, other):
        inverse = 1.0 / jnp.sum(sums[0], axis=0, keepdims=True)
        inner_row = jnp.sum(sums[1], axis=0, keepdims=True) * inverse
        spread = spread_of(number)
        next_spread = spread_of(following)
        next_sums = (zero, zero)
        out = jnp.zeros((2 * DH, 2 * BLK), F32)
        for g in range(9):
            next_sums = first_group(following, g, next_spread, next_sums, other)
            turned, mixed, heat = second_group(
                number, g, spread, inverse, inner_row, heat, buffer
            )
            if g % 2 == 0 and g < 8:
                waiting = turned, mixed
                continue
            if g % 2 == 1:
                turned = jnp.concatenate([waiting[0], turned], axis=1)
                mixed = jnp.concatenate([waiting[1], mixed], axis=0)
            out = out + dot_nn(turned, mixed)
        close(number, out)
        return next_sums, heat

    sums = (zero, zero)
    first_spread = spread_of(0)
    for g in range(9):
        sums = first_group(0, g, first_spread, sums, wbuf)

    def two_blocks(index, carry):
        sums, heat = carry
        number = index * 2
        sums, heat = step(number, number + 1, sums, heat, wbuf, wbuf2)
        following = jnp.minimum(number + 2, 15)
        return step(number + 1, following, sums, heat, wbuf2, wbuf)

    _, heat = lax.fori_loop(0, 8, two_blocks, (sums, zero))
    heat = jnp.sum(jnp.sum(heat, axis=0, keepdims=True), axis=1, keepdims=True)
    upper, lower = high_low(jnp.broadcast_to(heat, (1, BLK)))
    tail = jnp.concatenate([upper, lower, jnp.zeros((6, BLK), F32)], axis=0).astype(BF)
    for chunk in range(16):
        mq_out[chunk, BLK:, :] = tail
    leaving = [
        pltpu.make_async_copy(source, target, sems.at[4 + number])
        for number, (source, target) in enumerate(
            (
                (before_out, before_hbm), (after_out, after_hbm), (mq_out, mq_hbm),
                (mqt_out, mqt_hbm), (acc.at[:, 1], own_hbm),
            )
        )
    ]
    before_out[...] = acc[:, 0].astype(BF)
    leaving[0].start()
    after_out[...] = acc[:, 2].astype(BF)
    for copy in leaving[1:]:
        copy.start()
    for copy in leaving:
        copy.wait()


def early_kernel(site, mqt, near, far, out):
    query_part = jnp.zeros((DH, D), F32)
    proj_part = jnp.zeros((DH, D), F32)
    for which, source in ((site[0], near), (1 - site[0], far)):
        for half in range(2):
            rows = source[half * 4 : half * 4 + 4].reshape(4 * BLK, 2 * D)
            spots = [(half * 4 + k) * 2 + which for k in range(4)]
            mixed_t = jnp.concatenate([mqt[spot] for spot in spots], axis=1)
            proj_part = proj_part + dot_nn(mixed_t[:DH], rows[:, D:])
            query_part = query_part + dot_nn(mixed_t[DH:], rows[:, :D])
    out[...] = jnp.concatenate([query_part, proj_part], axis=0).astype(BF)


def head_kernel(
    site, own, low, high, kv, qb, early, mq, near, far, kv_out, parts_out, turned,
):
    core = site[0]
    for b in range(16):
        total = own[b] + low[b].astype(F32) + high[b].astype(F32)
        total_t = total.T
        key_t = kv[b].astype(F32).T[:DH]
        extra = qb[b, BLK:, :].astype(F32)
        factor = extra[3:4] + extra[4:5]
        grad_t = total_t[:DH]
        inside = jnp.sum(key_t * grad_t, axis=0, keepdims=True) * (1.0 / DH)
        joined = jnp.concatenate([(grad_t - key_t * inside) * factor, total_t[DH:]], axis=0)
        turned[b] = joined.astype(BF)
        target_x = jnp.bitwise_xor(site[1], b // 4)
        target_y = jnp.bitwise_xor(site[2], b % 4)
        kv_out[target_x, target_y] = joined.T.astype(BF)
    both_part = jnp.zeros((2 * DH, D), F32)
    for which, source in ((core, near), (1 - core, far)):
        for half in range(2):
            hidden = source[half * 4 : half * 4 + 4].reshape(4 * BLK, D)
            spots = [(half * 4 + k) * 2 + which for k in range(4)]
            both_t = jnp.concatenate([turned[spot] for spot in spots], axis=1)
            both_part = both_part + dot_nn(both_t, hidden)
    lines = []
    for row in (BLK, BLK + 1):
        pairs = [
            mq[seat(h, 0), row : row + 1].astype(F32) + mq[seat(h, 1), row : row + 1].astype(F32)
            for h in range(H)
        ]
        lines.append(0.5 * jnp.concatenate(pairs, axis=0))
    whole_sum = lines[0] + lines[1]
    upper, lower = high_low(whole_sum)
    extra = jnp.concatenate([upper, lower, upper, lower], axis=1).astype(BF)
    query_part, proj_part = early[:DH], early[DH:]
    joined = jnp.concatenate([query_part, both_part.astype(BF), proj_part], axis=0)
    for g in range(16):
        parts_out[g, :16] = joined[g * 16 : (g + 1) * 16]
        parts_out[g, 16:] = extra


def sum_kernel(arrived, share_out, temper_out):
    total = jnp.zeros((24, D), F32)
    for g in range(16):
        total = total + arrived[g].astype(F32)
    temper_out[...] = total[16:, :128] + total[16:, 128:256]
    share = total[:16].astype(BF)
    for k in range(64):
        share_out[k] = share


def output_kernel(core, near, far, gain, wq, wk, wv, gq, gk, gv, gp, gg, turned):
    for which, source in ((core[0], near), (1 - core[0], far)):
        for chip in range(64):
            gx, zl, tx, zh = chip // 16, chip // 8 % 2, chip // 2 % 4, chip % 2
            quarter = tx % 2 * 2 + zh
            start = pl.multiple_of(gx * 128 + which * 64 + quarter * 16, 16)
            turned[zl * 2 + tx // 2, pl.ds(start, 16), :] = source[chip]
    gp[...] = turned[3].astype(F32)
    total = jnp.zeros((D, 1), F32)
    for m, (out, weight) in enumerate(((gq, wq), (gk, wk), (gv, wv))):
        value = turned[m].T.astype(F32)
        out[...] = value
        total = total + jnp.sum(value * weight[...].astype(F32), axis=1, keepdims=True)
    line = jnp.broadcast_to(total, (D, 128)).T
    gg[...] = line[:1] / gain[...]


def finish_kernel(
    site, tok, gain, mq, kv0, kv1, kv2, kv3, wq, wk, wv, wp, layer_out, grad_tok, kv,
):
    for step_y, piece in enumerate((kv0, kv1, kv2, kv3)):
        for step_x in range(4):
            source_x = jnp.bitwise_xor(site[1], step_x)
            source_y = jnp.bitwise_xor(site[2], step_y)
            kv[source_x * 4 + source_y] = piece[step_x]

    def gathered(ref, lanes):
        halves = [
            jnp.concatenate([ref[seat(h, slot), :BLK, lanes] for h in range(H)], axis=1)
            for slot in range(2)
        ]
        return jnp.concatenate(halves, axis=0)

    left, right = slice(0, DH), slice(DH, 2 * DH)
    unit, factor_in, _ = normed_hidden(tok[...], gain[...])
    layer_out[...] = dot_nn(gathered(mq, left), wp[...]).astype(BF)
    query_d, key_d, value_d = gathered(mq, right), gathered(kv, left), gathered(kv, right)
    back_hidden = dot_nt(query_d, wq[...]) + dot_nt(key_d, wk[...]) + dot_nt(value_d, wv[...])
    slope_in = back_hidden * gain[...]
    grad_tok[...] = factor_in * (
        slope_in - unit * jnp.mean(slope_in * unit, axis=-1, keepdims=True)
    )


def whole(shape, dtype):
    return jax.ShapeDtypeStruct(shape, dtype)


def shift(block, step):
    spots = [(t % 2) * 8 + t // 2 for t in range(16)]
    return lax.ppermute(block, RING, [(spots[t], spots[(t + step) % 16]) for t in range(16)])


def swap_cores(block):
    return lax.ppermute(block, "cr", [(0, 1), (1, 0)])


def swap_near(block, axes, step):
    return lax.ppermute(block, axes, [(i, i ^ step) for i in range(4)])


def local(
    tokens, norm_gain, w_query, w_key, w_value, w_proj, temper, neighbours, valid_mask, cotangent
):
    tok = tokens.reshape(ROWS, D)
    cot = cotangent.reshape(ROWS, D)
    gain = norm_gain.reshape(1, D)
    core = lax.axis_index("cr")
    any_spec = pl.BlockSpec(memory_space=pl.ANY)
    smem = pl.BlockSpec(memory_space=pltpu.SMEM)
    hbm = pl.BlockSpec(memory_space=pltpu.HBM)
    vmem = pl.BlockSpec(memory_space=pltpu.VMEM)

    pair = (16, BLK, 2 * DH)
    wide = (16, BLK + EXTRA, 2 * DH)
    kv_send, factors = pl.pallas_call(
        key_kernel,
        cost_estimate=cost(3),
        out_shape=(whole(pair, BF), whole((ROWS, 128), F32)),
        compiler_params=params(56),
    )(tok, gain, w_key, w_value)
    qb_send, rows_send = pl.pallas_call(
        query_kernel,
        cost_estimate=cost(4),
        out_shape=(whole(wide, BF), whole((8, BLK, 2 * D), BF)),
        compiler_params=params(56),
    )(
        tok, gain, cot, neighbours.reshape(2, NB), valid_mask.reshape(2, NB), factors,
        w_query, w_proj,
    )

    own = lax.all_to_all(kv_send, GROUP, 0, 0, tiled=True)
    qb_send, own = lax.optimization_barrier((qb_send, own))
    before = shift(own, 1)
    after = shift(own, -1)
    qb = lax.all_to_all(qb_send, GROUP, 0, 0, tiled=True)
    rows_send, qb, before, after = lax.optimization_barrier((rows_send, qb, before, after))
    rows_near = lax.all_to_all(rows_send, ("gx", "zl"), 0, 0, tiled=True)
    head_id = lax.axis_index("gx") * 2 + core
    temp = temper[head_id] * SCALE
    coef = jnp.stack([temp * math.log2(math.e), temp])

    mq_send, mqt, own_grad, before_grad, after_grad = pl.pallas_call(
        attend_kernel,
        cost_estimate=cost(36),
        out_shape=(
            whole(wide, BF), whole((16, 2 * DH, BLK), BF), whole(pair, F32),
            whole(pair, BF), whole(pair, BF),
        ),
        in_specs=[smem] + [any_spec] * 3 + [vmem],
        out_specs=tuple([hbm] * 5),
        scratch_shapes=[
            pltpu.VMEM(wide, BF),
            pltpu.VMEM((16, 2 * DH, BLK), BF),
            pltpu.VMEM(pair, BF),
            pltpu.VMEM(pair, BF),
            pltpu.VMEM((16, 3, BLK, 2 * DH), BF),
            pltpu.VMEM((16, 2 * DH, 3 * BLK), BF),
            pltpu.VMEM((16, 3, BLK, 2 * DH), F32),
            pltpu.VMEM((NB * BLK, 2 * BLK), F32),
            pltpu.VMEM((NB * BLK, 2 * BLK), F32),
            pltpu.VMEM((16, 128), F32),
            pltpu.SMEM((16, 128), F32),
            pltpu.SemaphoreType.DMA((9,)),
        ],
        compiler_params=params(56),
    )(coef, own, before, after, qb)
    from_after = shift(before_grad, -1)
    from_before = shift(after_grad, 1)
    rows_near, mq_send = lax.optimization_barrier((rows_near, mq_send))
    rows_far = swap_cores(rows_near)
    mq = lax.all_to_all(mq_send, GROUP, 0, 0, tiled=True)
    site = jnp.stack([core, lax.axis_index("gx"), lax.axis_index("zl") * 2 + core])
    early = pl.pallas_call(
        early_kernel,
        cost_estimate=cost(3),
        out_shape=whole((2 * DH, D), BF),
        in_specs=[smem] + [vmem] * 3,
        compiler_params=params(10),
    )(site, mqt, rows_near, rows_far)
    hidden_spec = pl.BlockSpec((8, BLK, D), lambda i: (0, 0, 0))

    def one_spec(array):
        return pl.BlockSpec(array.shape, lambda i: (0,) * array.ndim)

    kv_back, parts = pl.pallas_call(
        head_kernel,
        cost_estimate=cost(7),
        out_shape=(whole((4, 4, BLK, 2 * DH), BF), whole((16, 24, D), BF)),
        grid=(1,),
        in_specs=[smem]
        + [one_spec(a) for a in (own_grad, from_after, from_before, own, qb, early, mq)]
        + [hidden_spec, hidden_spec],
        scratch_shapes=[pltpu.VMEM((16, 2 * DH, BLK), BF)],
        compiler_params=params(56),
    )(site, own_grad, from_after, from_before, own, qb, early, mq, rows_near, rows_far)
    arrived = lax.all_to_all(parts, RING, 0, 0, tiled=True)
    turn = [kv_back[0]] + [swap_near(kv_back[step], "gx", step) for step in range(1, 4)]
    arrived, *turn = lax.optimization_barrier((arrived, *turn))
    share, temper_sum = pl.pallas_call(
        sum_kernel,
        cost_estimate=cost(2),
        out_shape=(whole((64, 16, D), BF), whole((H, 128), F32)),
        compiler_params=params(6),
    )(arrived)
    near = lax.all_to_all(share, CHIPS, 0, 0, tiled=True)
    kv = [jnp.stack([piece[step] for piece in turn]) for step in range(4)]
    kv = [kv[0]] + [swap_near(kv[step], ("zl", "cr"), step) for step in range(1, 4)]
    near, *kv = lax.optimization_barrier((near, *kv))
    layer_out, grad_tokens = pl.pallas_call(
        finish_kernel,
        cost_estimate=cost(4),
        out_shape=(whole((ROWS, D), BF), whole((ROWS, D), F32)),
        in_specs=[smem] + [vmem] * 11,
        scratch_shapes=[pltpu.VMEM(pair, BF)],
        compiler_params=params(56),
    )(site, tok, gain, mq, *kv, w_query, w_key, w_value, w_proj)
    far = swap_cores(near)
    square = whole((D, D), F32)
    gq, gk, gv, gp, grad_gain = pl.pallas_call(
        output_kernel,
        cost_estimate=cost(5),
        out_shape=(square, square, square, square, whole((1, D), F32)),
        in_specs=[smem] + [vmem] * 6,
        scratch_shapes=[pltpu.VMEM((4, D, D), BF)],
        compiler_params=params(16),
    )(core.reshape(1), near, far, gain, w_query, w_key, w_value)
    grad_temper = temper_sum[:, 0] / (temper * math.log2(math.e))
    return (
        layer_out.reshape(tokens.shape),
        grad_tokens.reshape(tokens.shape),
        grad_gain.reshape(D),
        gq,
        gk,
        gv,
        gp,
        grad_temper,
    )


def solution(mesh):
    fine = Mesh(mesh.devices.reshape(4, 2, 2, 4, 2), ALL)
    lattice = ("gx", ("zl", "cr"), ("tx", "zh"))
    blocks = P(*lattice, None, None)
    lists = P(*lattice, None)
    return jax.shard_map(
        local,
        mesh=fine,
        in_specs=(blocks, P(), P(), P(), P(), P(), P(), lists, lists, blocks),
        out_specs=(blocks, blocks, P(), P(), P(), P(), P(), P()),
        check_vma=False,
    )
```

```python
import math

import jax
import jax.numpy as jnp
from jax import lax
from jax.experimental import pallas as pl
from jax.experimental.pallas import tpu as pltpu
from jax.sharding import Mesh, PartitionSpec as P

NORM_EPS = 1e-05
HEAD_EPS = 1e-06
D = 512
H = 8
DH = 64
BLK = 128
NB = 27
ROWS = 256
SCALE = DH**-0.5
BF = jnp.bfloat16
F32 = jnp.float32
GROUP = ("gx", "zl", "cr")
RING = ("zl", "tx", "zh")
CHIPS = ("gx", "zl", "tx", "zh")
ALL = ("gx", "zl", "cr", "tx", "zh")
EXTRA = 8
MIB = 1024 * 1024


def params(mebibytes):
    return pltpu.CompilerParams(vmem_limit_bytes=mebibytes * MIB)


def cost(micros):
    return pl.CostEstimate(
        flops=int(micros * 1e9), bytes_accessed=int(micros * 1e6), transcendentals=0
    )


def dot_nn(left, right):
    return jnp.dot(left, right, preferred_element_type=F32)


def dot_nt(left, right):
    return lax.dot_general(left, right, (((1,), (1,)), ((), ())), preferred_element_type=F32)


def dot_tn(left, right):
    return lax.dot_general(left, right, (((0,), (0,)), ((), ())), preferred_element_type=F32)


def head(values, index):
    return values[:, index * DH : (index + 1) * DH]


def normed_hidden(tokens, gain):
    values = tokens.astype(F32)
    factor = lax.rsqrt(jnp.mean(values * values, axis=-1, keepdims=True) + NORM_EPS)
    unit = values * factor
    return unit, factor, (unit * gain).astype(BF)


def high_low(values):
    upper = values.astype(BF).astype(F32)
    return upper, values - upper


def seat(h, slot):
    return (h // 2) * 4 + slot * 2 + h % 2


def key_kernel(tok, gain, wk, wv, kv_out, fac_out):
    _, _, hidden = normed_hidden(tok[...], gain[...])
    lane = lax.broadcasted_iota(jnp.int32, (ROWS, 128), 1)
    factors = jnp.zeros((ROWS, 128), F32)
    key_f = dot_nn(hidden, wk[...])
    value = dot_nn(hidden, wv[...]).astype(BF)
    for h in range(H):
        part = head(key_f, h)
        factor = lax.rsqrt(jnp.mean(part * part, axis=-1, keepdims=True) + HEAD_EPS)
        factors = jnp.where(lane == H + h, factor, factors)
        joined = jnp.concatenate([(part * factor).astype(BF), head(value, h)], axis=1)
        kv_out[seat(h, 0)] = joined[:BLK]
        kv_out[seat(h, 1)] = joined[BLK:]
    fac_out[...] = factors


def query_kernel(tok, gain, cot, neighbours, valid, factors_in, wq, wp, qb_out, rows_out):
    _, _, hidden = normed_hidden(tok[...], gain[...])
    for k in range(8):
        lines = slice((k % 2) * BLK, (k % 2 + 1) * BLK)
        rows_out[k, :, :D] = hidden[lines]
        rows_out[k, :, D:] = cot[lines]
    lane = lax.broadcasted_iota(jnp.int32, (ROWS, 128), 1)
    factors = factors_in[...]
    query_f = dot_nn(hidden, wq[...])
    back = dot_nt(cot[...], wp[...]).astype(BF)
    for h in range(H):
        part = head(query_f, h)
        factor = lax.rsqrt(jnp.mean(part * part, axis=-1, keepdims=True) + HEAD_EPS)
        factors = jnp.where(lane == h, factor, factors)
        joined = jnp.concatenate([(part * factor).astype(BF), head(back, h)], axis=1)
        qb_out[seat(h, 0), :BLK] = joined[:BLK]
        qb_out[seat(h, 1), :BLK] = joined[BLK:]
    ids = neighbours[...]
    keep = valid[...]
    place_y = lax.axis_index("zl") * 2 + lax.axis_index("cr")
    place_t = (lax.axis_index("tx") * 2 + lax.axis_index("zh")) * 2
    own_t = place_t + lax.broadcasted_iota(jnp.int32, (2, NB), 0)
    step_t = jnp.bitwise_and(ids - own_t + 1, 15)
    step_y = jnp.bitwise_and(jnp.right_shift(ids, 4) - place_y + 1, 3)
    step_x = jnp.bitwise_and(jnp.right_shift(ids, 6) - lax.axis_index("gx") + 1, 3)
    slots = step_x * 9 + step_y * 3 + step_t
    short = lax.broadcasted_iota(jnp.int32, (2, 128), 1)
    kept = jnp.zeros((2, 128), F32)
    for slot in range(NB):
        hit = short == slots[:, slot : slot + 1]
        kept = kept + jnp.where(hit, keep[:, slot : slot + 1].astype(F32), 0.0)
    turned = factors.T
    for h in range(H):
        for slot in range(2):
            lanes = slice(slot * BLK, (slot + 1) * BLK)
            rows = [kept[slot : slot + 1]]
            rows += list(high_low(turned[h : h + 1, lanes]))
            rows += list(high_low(turned[H + h : H + h + 1, lanes]))
            rows.append(jnp.zeros((3, 128), F32))
            qb_out[seat(h, slot), BLK:] = jnp.concatenate(rows, axis=0).astype(BF)


def attend_kernel(
    coef, own, before, after, qb, mq_hbm, mqt_hbm, own_hbm, before_hbm, after_hbm,
    mq_out, mqt_out, before_out, after_out, kvall, kvt, acc, wbuf, wbuf2, keep_rows, keep, sems,
):
    copies = []
    for number, src in enumerate((before, own, after)):
        copies.append(pltpu.make_async_copy(src, kvall.at[:, number], sems.at[number]))
    for copy in copies:
        copy.start()
    for number in range(16):
        keep_rows[number : number + 1] = qb[number, BLK:, :].astype(F32)[:1]
    copies.append(pltpu.make_async_copy(keep_rows, keep, sems.at[3]))
    copies[3].start()
    acc[...] = jnp.zeros_like(acc)
    for copy in copies:
        copy.wait()
    for place in range(16):
        for t in range(3):
            kvt[place, :, t * BLK : (t + 1) * BLK] = kvall[place, t].T

    exp_coef = coef[0]
    grad_coef = coef[1]
    lane = lax.broadcasted_iota(jnp.int32, (BLK, 2 * DH), 1)
    low = (lane < DH).astype(F32).astype(BF)
    high = (lane >= DH).astype(F32).astype(BF)

    def fold(values):
        return jnp.sum(values.reshape(-1, 8, BLK), axis=0)

    def spread_of(number):
        both = qb[number, :BLK, :]
        return jnp.concatenate([both * low, both * high], axis=0)

    def place_of(number, g):
        return (number // 4 + g // 3 + 3) % 4 * 4 + (number % 4 + g % 3 + 3) % 4

    def first_group(number, g, spread, sums, buffer):
        keys = kvall[place_of(number, g)].reshape(3 * BLK, 2 * DH)
        pair = dot_nt(keys, spread)
        total, inner = sums
        for k in range(3):
            score = pair[k * BLK : (k + 1) * BLK, :BLK] * exp_coef
            slope = pair[k * BLK : (k + 1) * BLK, BLK:]
            weight = jnp.exp2(score)
            slot = g * 3 + k
            kept = keep[number, slot]
            total = total + fold(weight) * kept
            inner = inner + fold(weight * slope) * kept
            base = (g * 3 + k) * BLK
            buffer[base : base + BLK, :BLK] = score
            buffer[base : base + BLK, BLK:] = slope
        return total, inner

    def second_group(number, g, spread, inverse, inner_row, heat, buffer):
        place = place_of(number, g)
        pieces = []
        for k in range(3):
            slot = g * 3 + k
            base = slot * BLK
            score = buffer[base : base + BLK, :BLK]
            prob = jnp.exp2(score) * (inverse * keep[number, slot])
            slope = buffer[base : base + BLK, BLK:]
            grad = prob * (slope - inner_row)
            heat = heat + fold(grad * score)
            scaled = grad * grad_coef
            pieces.append(jnp.concatenate([scaled.astype(BF), prob.astype(BF)], axis=1))
        mixed = jnp.concatenate(pieces, axis=0)
        acc[place] += dot_nn(mixed, spread).reshape(3, BLK, 2 * DH)
        return kvt[place], mixed, heat

    def close(number, out):
        extra = qb[number, BLK:, :].astype(F32)
        factor = extra[1:2] + extra[2:3]
        query_t = qb[number, :BLK, :].astype(F32).T[:DH]
        grad_t = out[:DH, :BLK]
        inside = jnp.sum(query_t * grad_t, axis=0, keepdims=True)
        query_d = (grad_t - query_t * (inside * (1.0 / DH))) * factor
        joined = jnp.concatenate([out[DH:, BLK:], query_d], axis=0)
        mq_out[number, :BLK, :] = joined.T.astype(BF)
        mqt_out[number] = joined.astype(BF)

    zero = jnp.zeros((8, BLK), F32)

    def step(number, following, sums, heat, buffer, other):
        inverse = 1.0 / jnp.sum(sums[0], axis=0, keepdims=True)
        inner_row = jnp.sum(sums[1], axis=0, keepdims=True) * inverse
        spread = spread_of(number)
        next_spread = None if following is None else spread_of(following)
        next_sums = (zero, zero)
        out = jnp.zeros((2 * DH, 2 * BLK), F32)
        for g in range(9):
            if following is not None:
                next_sums = first_group(following, g, next_spread, next_sums, other)
            turned, mixed, heat = second_group(
                number, g, spread, inverse, inner_row, heat, buffer
            )
            if g % 2 == 0 and g < 8:
                waiting = turned, mixed
                continue
            if g % 2 == 1:
                turned = jnp.concatenate([waiting[0], turned], axis=1)
                mixed = jnp.concatenate([waiting[1], mixed], axis=0)
            out = out + dot_nn(turned, mixed)
        close(number, out)
        return next_sums, heat

    sums = (zero, zero)
    first_spread = spread_of(0)
    for g in range(9):
        sums = first_group(0, g, first_spread, sums, wbuf)

    def two_blocks(index, carry):
        sums, heat = carry
        number = index * 2
        sums, heat = step(number, number + 1, sums, heat, wbuf, wbuf2)
        return step(number + 1, number + 2, sums, heat, wbuf2, wbuf)

    sums, heat = lax.fori_loop(0, 7, two_blocks, (sums, zero))
    sums, heat = step(14, 15, sums, heat, wbuf, wbuf2)
    _, heat = step(15, None, sums, heat, wbuf2, wbuf)
    heat = jnp.sum(jnp.sum(heat, axis=0, keepdims=True), axis=1, keepdims=True)
    upper, lower = high_low(jnp.broadcast_to(heat, (1, BLK)))
    tail = jnp.concatenate([upper, lower, jnp.zeros((6, BLK), F32)], axis=0).astype(BF)
    for chunk in range(16):
        mq_out[chunk, BLK:, :] = tail
    leaving = [
        pltpu.make_async_copy(source, target, sems.at[4 + number])
        for number, (source, target) in enumerate(
            (
                (before_out, before_hbm), (after_out, after_hbm), (mq_out, mq_hbm),
                (mqt_out, mqt_hbm), (acc.at[:, 1], own_hbm),
            )
        )
    ]
    before_out[...] = acc[:, 0].astype(BF)
    leaving[0].start()
    after_out[...] = acc[:, 2].astype(BF)
    for copy in leaving[1:]:
        copy.start()
    for copy in leaving:
        copy.wait()


def early_kernel(site, mqt, near, far, out):
    query_part = jnp.zeros((DH, D), F32)
    proj_part = jnp.zeros((DH, D), F32)
    for which, source in ((site[0], near), (1 - site[0], far)):
        for half in range(2):
            rows = source[half * 4 : half * 4 + 4].reshape(4 * BLK, 2 * D)
            spots = [(half * 4 + k) * 2 + which for k in range(4)]
            mixed_t = jnp.concatenate([mqt[spot] for spot in spots], axis=1)
            proj_part = proj_part + dot_nn(mixed_t[:DH], rows[:, D:])
            query_part = query_part + dot_nn(mixed_t[DH:], rows[:, :D])
    out[...] = jnp.concatenate([query_part, proj_part], axis=0).astype(BF)


def head_kernel(
    site, own, low, high, kv, qb, early, mq, near, far, kv_out, parts_out, turned,
):
    core = site[0]
    for b in range(16):
        total = own[b] + low[b].astype(F32) + high[b].astype(F32)
        total_t = total.T
        key_t = kv[b].astype(F32).T[:DH]
        extra = qb[b, BLK:, :].astype(F32)
        factor = extra[3:4] + extra[4:5]
        grad_t = total_t[:DH]
        inside = jnp.sum(key_t * grad_t, axis=0, keepdims=True) * (1.0 / DH)
        joined = jnp.concatenate([(grad_t - key_t * inside) * factor, total_t[DH:]], axis=0)
        turned[b] = joined.astype(BF)
        target_x = jnp.bitwise_xor(site[1], b // 4)
        target_y = jnp.bitwise_xor(site[2], b % 4)
        kv_out[target_x, target_y] = joined.T.astype(BF)
    both_part = jnp.zeros((2 * DH, D), F32)
    for which, source in ((core, near), (1 - core, far)):
        for half in range(2):
            hidden = source[half * 4 : half * 4 + 4].reshape(4 * BLK, D)
            spots = [(half * 4 + k) * 2 + which for k in range(4)]
            both_t = jnp.concatenate([turned[spot] for spot in spots], axis=1)
            both_part = both_part + dot_nn(both_t, hidden)
    lines = []
    for row in (BLK, BLK + 1):
        pairs = [
            mq[seat(h, 0), row : row + 1].astype(F32) + mq[seat(h, 1), row : row + 1].astype(F32)
            for h in range(H)
        ]
        lines.append(0.5 * jnp.concatenate(pairs, axis=0))
    whole_sum = lines[0] + lines[1]
    upper, lower = high_low(whole_sum)
    extra = jnp.concatenate([upper[:, :DH], lower[:, DH:]], axis=1).astype(BF)
    query_part, proj_part = early[:DH], early[DH:]
    joined = jnp.concatenate([query_part, both_part.astype(BF), proj_part], axis=0)
    for g in range(16):
        for c in range(4):
            parts_out[g, c * 16 : (c + 1) * 16] = joined[
                g * 16 : (g + 1) * 16, c * 128 : (c + 1) * 128
            ]
        parts_out[g, 64:] = extra


def sum_kernel(arrived, share_out, temper_out):
    total = jnp.zeros((72, 128), F32)
    for g in range(16):
        total = total + arrived[g].astype(F32)
    temper_out[...] = jnp.broadcast_to(total[64:, :1] + total[64:, DH : DH + 1], (H, 128))
    share = jnp.concatenate([total[c * 16 : (c + 1) * 16] for c in range(4)], axis=1).astype(BF)
    for k in range(64):
        share_out[k] = share


def output_kernel(core, near, far, gain, wq, wk, wv, gq, gk, gv, gp, gg, turned):
    for which, source in ((core[0], near), (1 - core[0], far)):
        for chip in range(64):
            gx, zl, tx, zh = chip // 16, chip // 8 % 2, chip // 2 % 4, chip % 2
            quarter = tx % 2 * 2 + zh
            start = pl.multiple_of(gx * 128 + which * 64 + quarter * 16, 16)
            turned[zl * 2 + tx // 2, pl.ds(start, 16), :] = source[chip]
    gp[...] = turned[3].astype(F32)
    total = jnp.zeros((D, 1), F32)
    for m, (out, weight) in enumerate(((gq, wq), (gk, wk), (gv, wv))):
        value = turned[m].T.astype(F32)
        out[...] = value
        total = total + jnp.sum(value * weight[...].astype(F32), axis=1, keepdims=True)
    line = jnp.broadcast_to(total, (D, 128)).T
    gg[...] = line[:1] / gain[...]


def finish_kernel(
    site, tok, gain, mq, kv0, kv1, kv2, kv3, wq, wk, wv, wp, layer_out, grad_tok, kv,
):
    for step_y, piece in enumerate((kv0, kv1, kv2, kv3)):
        for step_x in range(4):
            source_x = jnp.bitwise_xor(site[1], step_x)
            source_y = jnp.bitwise_xor(site[2], step_y)
            kv[source_x * 4 + source_y] = piece[step_x]

    def gathered(ref, lanes):
        halves = [
            jnp.concatenate([ref[seat(h, slot), :BLK, lanes] for h in range(H)], axis=1)
            for slot in range(2)
        ]
        return jnp.concatenate(halves, axis=0)

    left, right = slice(0, DH), slice(DH, 2 * DH)
    unit, factor_in, _ = normed_hidden(tok[...], gain[...])
    layer_out[...] = dot_nn(gathered(mq, left), wp[...]).astype(BF)
    query_d, key_d, value_d = gathered(mq, right), gathered(kv, left), gathered(kv, right)
    back_hidden = dot_nt(query_d, wq[...]) + dot_nt(key_d, wk[...]) + dot_nt(value_d, wv[...])
    slope_in = back_hidden * gain[...]
    grad_tok[...] = factor_in * (
        slope_in - unit * jnp.mean(slope_in * unit, axis=-1, keepdims=True)
    )


def whole(shape, dtype):
    return jax.ShapeDtypeStruct(shape, dtype)


def shift(block, step):
    spots = [(t % 2) * 8 + t // 2 for t in range(16)]
    return lax.ppermute(block, RING, [(spots[t], spots[(t + step) % 16]) for t in range(16)])


def swap_cores(block):
    return lax.ppermute(block, "cr", [(0, 1), (1, 0)])


def swap_near(block, axes, step):
    return lax.ppermute(block, axes, [(i, i ^ step) for i in range(4)])


def local(
    tokens, norm_gain, w_query, w_key, w_value, w_proj, temper, neighbours, valid_mask, cotangent
):
    tok = tokens.reshape(ROWS, D)
    cot = cotangent.reshape(ROWS, D)
    gain = norm_gain.reshape(1, D)
    core = lax.axis_index("cr")
    any_spec = pl.BlockSpec(memory_space=pl.ANY)
    smem = pl.BlockSpec(memory_space=pltpu.SMEM)
    hbm = pl.BlockSpec(memory_space=pltpu.HBM)
    vmem = pl.BlockSpec(memory_space=pltpu.VMEM)

    pair = (16, BLK, 2 * DH)
    wide = (16, BLK + EXTRA, 2 * DH)
    kv_send, factors = pl.pallas_call(
        key_kernel,
        cost_estimate=cost(3),
        out_shape=(whole(pair, BF), whole((ROWS, 128), F32)),
        compiler_params=params(56),
    )(tok, gain, w_key, w_value)
    qb_send, rows_send = pl.pallas_call(
        query_kernel,
        cost_estimate=cost(4),
        out_shape=(whole(wide, BF), whole((8, BLK, 2 * D), BF)),
        compiler_params=params(56),
    )(
        tok, gain, cot, neighbours.reshape(2, NB), valid_mask.reshape(2, NB), factors,
        w_query, w_proj,
    )

    own = lax.all_to_all(kv_send, GROUP, 0, 0, tiled=True)
    qb_send, own = lax.optimization_barrier((qb_send, own))
    before = shift(own, 1)
    after = shift(own, -1)
    qb = lax.all_to_all(qb_send, GROUP, 0, 0, tiled=True)
    rows_send, qb, before, after = lax.optimization_barrier((rows_send, qb, before, after))
    rows_near = lax.all_to_all(rows_send, ("gx", "zl"), 0, 0, tiled=True)
    head_id = lax.axis_index("gx") * 2 + core
    temp = temper[head_id] * SCALE
    coef = jnp.stack([temp * math.log2(math.e), temp])

    mq_send, mqt, own_grad, before_grad, after_grad = pl.pallas_call(
        attend_kernel,
        cost_estimate=cost(36),
        out_shape=(
            whole(wide, BF), whole((16, 2 * DH, BLK), BF), whole(pair, F32),
            whole(pair, BF), whole(pair, BF),
        ),
        in_specs=[smem] + [any_spec] * 3 + [vmem],
        out_specs=tuple([hbm] * 5),
        scratch_shapes=[
            pltpu.VMEM(wide, BF),
            pltpu.VMEM((16, 2 * DH, BLK), BF),
            pltpu.VMEM(pair, BF),
            pltpu.VMEM(pair, BF),
            pltpu.VMEM((16, 3, BLK, 2 * DH), BF),
            pltpu.VMEM((16, 2 * DH, 3 * BLK), BF),
            pltpu.VMEM((16, 3, BLK, 2 * DH), F32),
            pltpu.VMEM((NB * BLK, 2 * BLK), F32),
            pltpu.VMEM((NB * BLK, 2 * BLK), F32),
            pltpu.VMEM((16, 128), F32),
            pltpu.SMEM((16, 128), F32),
            pltpu.SemaphoreType.DMA((9,)),
        ],
        compiler_params=params(60),
    )(coef, own, before, after, qb)
    from_after = shift(before_grad, -1)
    from_before = shift(after_grad, 1)
    rows_near, mq_send = lax.optimization_barrier((rows_near, mq_send))
    rows_far = swap_cores(rows_near)
    mq = lax.all_to_all(mq_send, GROUP, 0, 0, tiled=True)
    site = jnp.stack([core, lax.axis_index("gx"), lax.axis_index("zl") * 2 + core])
    early = pl.pallas_call(
        early_kernel,
        cost_estimate=cost(3),
        out_shape=whole((2 * DH, D), BF),
        in_specs=[smem] + [vmem] * 3,
        compiler_params=params(10),
    )(site, mqt, rows_near, rows_far)
    hidden_spec = pl.BlockSpec((8, BLK, D), lambda i: (0, 0, 0))

    def one_spec(array):
        return pl.BlockSpec(array.shape, lambda i: (0,) * array.ndim)

    kv_back, parts = pl.pallas_call(
        head_kernel,
        cost_estimate=cost(7),
        out_shape=(whole((4, 4, BLK, 2 * DH), BF), whole((16, 72, 128), BF)),
        grid=(1,),
        in_specs=[smem]
        + [one_spec(a) for a in (own_grad, from_after, from_before, own, qb, early, mq)]
        + [hidden_spec, hidden_spec],
        scratch_shapes=[pltpu.VMEM((16, 2 * DH, BLK), BF)],
        compiler_params=params(56),
    )(site, own_grad, from_after, from_before, own, qb, early, mq, rows_near, rows_far)
    arrived = lax.all_to_all(parts, RING, 0, 0, tiled=True)
    turn = [kv_back[0]] + [swap_near(kv_back[step], "gx", step) for step in range(1, 4)]
    share, temper_sum = pl.pallas_call(
        sum_kernel,
        cost_estimate=cost(2),
        out_shape=(whole((64, 16, D), BF), whole((H, 128), F32)),
        compiler_params=params(6),
    )(arrived)
    near = lax.all_to_all(share, CHIPS, 0, 0, tiled=True)
    kv = [jnp.stack([piece[step] for piece in turn]) for step in range(4)]
    kv = [kv[0]] + [swap_near(kv[step], ("zl", "cr"), step) for step in range(1, 4)]
    near, *kv = lax.optimization_barrier((near, *kv))
    layer_out, grad_tokens = pl.pallas_call(
        finish_kernel,
        cost_estimate=cost(4),
        out_shape=(whole((ROWS, D), BF), whole((ROWS, D), F32)),
        in_specs=[smem] + [vmem] * 11,
        scratch_shapes=[pltpu.VMEM(pair, BF)],
        compiler_params=params(56),
    )(site, tok, gain, mq, *kv, w_query, w_key, w_value, w_proj)
    far = swap_cores(near)
    square = whole((D, D), F32)
    gq, gk, gv, gp, grad_gain = pl.pallas_call(
        output_kernel,
        cost_estimate=cost(5),
        out_shape=(square, square, square, square, whole((1, D), F32)),
        in_specs=[smem] + [vmem] * 6,
        scratch_shapes=[pltpu.VMEM((4, D, D), BF)],
        compiler_params=params(16),
    )(core.reshape(1), near, far, gain, w_query, w_key, w_value)
    grad_temper = temper_sum[:, 0] / (temper * math.log2(math.e))
    return (
        layer_out.reshape(tokens.shape),
        grad_tokens.reshape(tokens.shape),
        grad_gain.reshape(D),
        gq,
        gk,
        gv,
        gp,
        grad_temper,
    )


def solution(mesh):
    fine = Mesh(mesh.devices.reshape(4, 2, 2, 4, 2), ALL)
    lattice = ("gx", ("zl", "cr"), ("tx", "zh"))
    blocks = P(*lattice, None, None)
    lists = P(*lattice, None)
    return jax.shard_map(
        local,
        mesh=fine,
        in_specs=(blocks, P(), P(), P(), P(), P(), P(), lists, lists, blocks),
        out_specs=(blocks, blocks, P(), P(), P(), P(), P(), P()),
        check_vma=False,
    )
```

```python
import math

import jax
import jax.numpy as jnp
from jax import lax
from jax.experimental import pallas as pl
from jax.experimental.pallas import tpu as pltpu
from jax.sharding import Mesh, PartitionSpec as P

NORM_EPS = 1e-05
HEAD_EPS = 1e-06
D = 512
H = 8
DH = 64
BLK = 128
NB = 27
ROWS = 256
SCALE = DH**-0.5
BF = jnp.bfloat16
F32 = jnp.float32
GROUP = ("gx", "zl", "cr")
RING = ("zl", "tx", "zh")
CHIPS = ("gx", "zl", "tx", "zh")
ALL = ("gx", "zl", "cr", "tx", "zh")
EXTRA = 8
MIB = 1024 * 1024


def params(mebibytes):
    return pltpu.CompilerParams(vmem_limit_bytes=mebibytes * MIB)


def cost(micros):
    return pl.CostEstimate(
        flops=int(micros * 1e9), bytes_accessed=int(micros * 1e6), transcendentals=0
    )


def dot_nn(left, right):
    return jnp.dot(left, right, preferred_element_type=F32)


def dot_nt(left, right):
    return lax.dot_general(left, right, (((1,), (1,)), ((), ())), preferred_element_type=F32)


def dot_tn(left, right):
    return lax.dot_general(left, right, (((0,), (0,)), ((), ())), preferred_element_type=F32)


def head(values, index):
    return values[:, index * DH : (index + 1) * DH]


def normed_hidden(tokens, gain):
    values = tokens.astype(F32)
    factor = lax.rsqrt(jnp.mean(values * values, axis=-1, keepdims=True) + NORM_EPS)
    unit = values * factor
    return unit, factor, (unit * gain).astype(BF)


def high_low(values):
    upper = values.astype(BF).astype(F32)
    return upper, values - upper


def seat(h, slot):
    return (h // 2) * 4 + slot * 2 + h % 2


def key_kernel(tok, gain, wk, wv, kv_out, fac_out):
    _, _, hidden = normed_hidden(tok[...], gain[...])
    lane = lax.broadcasted_iota(jnp.int32, (ROWS, 128), 1)
    factors = jnp.zeros((ROWS, 128), F32)
    key_f = dot_nn(hidden, wk[...])
    value = dot_nn(hidden, wv[...]).astype(BF)
    for h in range(H):
        part = head(key_f, h)
        factor = lax.rsqrt(jnp.mean(part * part, axis=-1, keepdims=True) + HEAD_EPS)
        factors = jnp.where(lane == H + h, factor, factors)
        joined = jnp.concatenate([(part * factor).astype(BF), head(value, h)], axis=1)
        kv_out[seat(h, 0)] = joined[:BLK]
        kv_out[seat(h, 1)] = joined[BLK:]
    fac_out[...] = factors


def query_kernel(tok, gain, cot, neighbours, valid, factors_in, wq, wp, qb_out, rows_out):
    _, _, hidden = normed_hidden(tok[...], gain[...])
    for k in range(8):
        lines = slice((k % 2) * BLK, (k % 2 + 1) * BLK)
        rows_out[k, :, :D] = hidden[lines]
        rows_out[k, :, D:] = cot[lines]
    lane = lax.broadcasted_iota(jnp.int32, (ROWS, 128), 1)
    factors = factors_in[...]
    query_f = dot_nn(hidden, wq[...])
    back = dot_nt(cot[...], wp[...]).astype(BF)
    for h in range(H):
        part = head(query_f, h)
        factor = lax.rsqrt(jnp.mean(part * part, axis=-1, keepdims=True) + HEAD_EPS)
        factors = jnp.where(lane == h, factor, factors)
        joined = jnp.concatenate([(part * factor).astype(BF), head(back, h)], axis=1)
        qb_out[seat(h, 0), :BLK] = joined[:BLK]
        qb_out[seat(h, 1), :BLK] = joined[BLK:]
    ids = neighbours[...]
    keep = valid[...]
    place_y = lax.axis_index("zl") * 2 + lax.axis_index("cr")
    place_t = (lax.axis_index("tx") * 2 + lax.axis_index("zh")) * 2
    own_t = place_t + lax.broadcasted_iota(jnp.int32, (2, NB), 0)
    step_t = jnp.bitwise_and(ids - own_t + 1, 15)
    step_y = jnp.bitwise_and(jnp.right_shift(ids, 4) - place_y + 1, 3)
    step_x = jnp.bitwise_and(jnp.right_shift(ids, 6) - lax.axis_index("gx") + 1, 3)
    slots = step_x * 9 + step_y * 3 + step_t
    short = lax.broadcasted_iota(jnp.int32, (2, 128), 1)
    kept = jnp.zeros((2, 128), F32)
    for slot in range(NB):
        hit = short == slots[:, slot : slot + 1]
        kept = kept + jnp.where(hit, keep[:, slot : slot + 1].astype(F32), 0.0)
    turned = factors.T
    for h in range(H):
        for slot in range(2):
            lanes = slice(slot * BLK, (slot + 1) * BLK)
            rows = [kept[slot : slot + 1]]
            rows += list(high_low(turned[h : h + 1, lanes]))
            rows += list(high_low(turned[H + h : H + h + 1, lanes]))
            rows.append(jnp.zeros((3, 128), F32))
            qb_out[seat(h, slot), BLK:] = jnp.concatenate(rows, axis=0).astype(BF)


def attend_kernel(
    coef, own, before, after, qb, mq_hbm, mqt_hbm, own_hbm, before_hbm, after_hbm,
    mq_out, mqt_out, before_out, after_out, kvall, kvt, acc, wbuf, wbuf2, keep_rows, keep, sems,
):
    copies = []
    for number, src in enumerate((before, own, after)):
        copies.append(pltpu.make_async_copy(src, kvall.at[:, number], sems.at[number]))
    for copy in copies:
        copy.start()
    for number in range(16):
        keep_rows[number : number + 1] = qb[number, BLK:, :].astype(F32)[:1]
    copies.append(pltpu.make_async_copy(keep_rows, keep, sems.at[3]))
    copies[3].start()
    acc[...] = jnp.zeros_like(acc)
    for copy in copies:
        copy.wait()
    for place in range(16):
        for t in range(3):
            kvt[place, :, t * BLK : (t + 1) * BLK] = kvall[place, t].T

    exp_coef = coef[0]
    grad_coef = coef[1]
    lane = lax.broadcasted_iota(jnp.int32, (BLK, 2 * DH), 1)
    low = (lane < DH).astype(F32).astype(BF)
    high = (lane >= DH).astype(F32).astype(BF)

    def fold(values):
        return jnp.sum(values.reshape(-1, 8, BLK), axis=0)

    def spread_of(number):
        both = qb[number, :BLK, :]
        return jnp.concatenate([both * low, both * high], axis=0)

    def place_of(number, g):
        return (number // 4 + g // 3 + 3) % 4 * 4 + (number % 4 + g % 3 + 3) % 4

    def first_group(number, g, spread, sums, buffer):
        keys = kvall[place_of(number, g)].reshape(3 * BLK, 2 * DH)
        pair = dot_nt(keys, spread)
        total, inner = sums
        for k in range(3):
            score = pair[k * BLK : (k + 1) * BLK, :BLK] * exp_coef
            slope = pair[k * BLK : (k + 1) * BLK, BLK:]
            weight = jnp.exp2(score)
            slot = g * 3 + k
            kept = keep[number, slot]
            total = total + fold(weight) * kept
            inner = inner + fold(weight * slope) * kept
            base = (g * 3 + k) * BLK
            buffer[base : base + BLK, :BLK] = score
            buffer[base : base + BLK, BLK:] = slope
        return total, inner

    def second_group(number, g, spread, inverse, inner_row, heat, buffer):
        place = place_of(number, g)
        pieces = []
        for k in range(3):
            slot = g * 3 + k
            base = slot * BLK
            score = buffer[base : base + BLK, :BLK]
            prob = jnp.exp2(score) * (inverse * keep[number, slot])
            slope = buffer[base : base + BLK, BLK:]
            grad = prob * (slope - inner_row)
            heat = heat + fold(grad * score)
            scaled = grad * grad_coef
            pieces.append(jnp.concatenate([scaled.astype(BF), prob.astype(BF)], axis=1))
        mixed = jnp.concatenate(pieces, axis=0)
        acc[place] += dot_nn(mixed, spread).reshape(3, BLK, 2 * DH)
        return kvt[place], mixed, heat

    def close(number, out):
        extra = qb[number, BLK:, :].astype(F32)
        factor = extra[1:2] + extra[2:3]
        query_t = qb[number, :BLK, :].astype(F32).T[:DH]
        grad_t = out[:DH, :BLK]
        inside = jnp.sum(query_t * grad_t, axis=0, keepdims=True)
        query_d = (grad_t - query_t * (inside * (1.0 / DH))) * factor
        joined = jnp.concatenate([out[DH:, BLK:], query_d], axis=0)
        mq_out[number, :BLK, :] = joined.T.astype(BF)
        mqt_out[number] = joined.astype(BF)

    zero = jnp.zeros((8, BLK), F32)

    def step(number, following, sums, heat, buffer, other):
        inverse = 1.0 / jnp.sum(sums[0], axis=0, keepdims=True)
        inner_row = jnp.sum(sums[1], axis=0, keepdims=True) * inverse
        spread = spread_of(number)
        next_spread = None if following is None else spread_of(following)
        next_sums = (zero, zero)
        out = jnp.zeros((2 * DH, 2 * BLK), F32)
        for g in range(9):
            if following is not None:
                next_sums = first_group(following, g, next_spread, next_sums, other)
            turned, mixed, heat = second_group(
                number, g, spread, inverse, inner_row, heat, buffer
            )
            if g % 2 == 0 and g < 8:
                waiting = turned, mixed
                continue
            if g % 2 == 1:
                turned = jnp.concatenate([waiting[0], turned], axis=1)
                mixed = jnp.concatenate([waiting[1], mixed], axis=0)
            out = out + dot_nn(turned, mixed)
        close(number, out)
        return next_sums, heat

    sums = (zero, zero)
    first_spread = spread_of(0)
    for g in range(9):
        sums = first_group(0, g, first_spread, sums, wbuf)

    def two_blocks(index, carry):
        sums, heat = carry
        number = index * 2
        sums, heat = step(number, number + 1, sums, heat, wbuf, wbuf2)
        return step(number + 1, number + 2, sums, heat, wbuf2, wbuf)

    sums, heat = lax.fori_loop(0, 7, two_blocks, (sums, zero))
    sums, heat = step(14, 15, sums, heat, wbuf, wbuf2)
    _, heat = step(15, None, sums, heat, wbuf2, wbuf)
    heat = jnp.sum(jnp.sum(heat, axis=0, keepdims=True), axis=1, keepdims=True)
    upper, lower = high_low(jnp.broadcast_to(heat, (1, BLK)))
    tail = jnp.concatenate([upper, lower, jnp.zeros((6, BLK), F32)], axis=0).astype(BF)
    for chunk in range(16):
        mq_out[chunk, BLK:, :] = tail
    leaving = [
        pltpu.make_async_copy(source, target, sems.at[4 + number])
        for number, (source, target) in enumerate(
            (
                (before_out, before_hbm), (after_out, after_hbm), (mq_out, mq_hbm),
                (mqt_out, mqt_hbm), (acc.at[:, 1], own_hbm),
            )
        )
    ]
    before_out[...] = acc[:, 0].astype(BF)
    leaving[0].start()
    after_out[...] = acc[:, 2].astype(BF)
    for copy in leaving[1:]:
        copy.start()
    for copy in leaving:
        copy.wait()


def early_kernel(site, mqt, near, far, out):
    query_part = jnp.zeros((DH, D), F32)
    proj_part = jnp.zeros((DH, D), F32)
    for which, source in ((site[0], near), (1 - site[0], far)):
        for half in range(2):
            rows = source[half * 4 : half * 4 + 4].reshape(4 * BLK, 2 * D)
            spots = [(half * 4 + k) * 2 + which for k in range(4)]
            mixed_t = jnp.concatenate([mqt[spot] for spot in spots], axis=1)
            proj_part = proj_part + dot_nn(mixed_t[:DH], rows[:, D:])
            query_part = query_part + dot_nn(mixed_t[DH:], rows[:, :D])
    out[...] = jnp.concatenate([query_part, proj_part], axis=0).astype(BF)


def head_kernel(
    site, own, low, high, kv, qb, early, mq, near, far, kv_out, parts_out, turned,
):
    core = site[0]
    for b in range(16):
        total = own[b] + low[b].astype(F32) + high[b].astype(F32)
        total_t = total.T
        key_t = kv[b].astype(F32).T[:DH]
        extra = qb[b, BLK:, :].astype(F32)
        factor = extra[3:4] + extra[4:5]
        grad_t = total_t[:DH]
        inside = jnp.sum(key_t * grad_t, axis=0, keepdims=True) * (1.0 / DH)
        joined = jnp.concatenate([(grad_t - key_t * inside) * factor, total_t[DH:]], axis=0)
        turned[b] = joined.astype(BF)
        target_x = jnp.bitwise_xor(site[1], b // 4)
        target_y = jnp.bitwise_xor(site[2], b % 4)
        kv_out[target_x, target_y] = joined.T.astype(BF)
    both_part = jnp.zeros((2 * DH, D), F32)
    for which, source in ((core, near), (1 - core, far)):
        for half in range(2):
            hidden = source[half * 4 : half * 4 + 4].reshape(4 * BLK, D)
            spots = [(half * 4 + k) * 2 + which for k in range(4)]
            both_t = jnp.concatenate([turned[spot] for spot in spots], axis=1)
            both_part = both_part + dot_nn(both_t, hidden)
    lines = []
    for row in (BLK, BLK + 1):
        pairs = [
            mq[seat(h, 0), row : row + 1].astype(F32) + mq[seat(h, 1), row : row + 1].astype(F32)
            for h in range(H)
        ]
        lines.append(0.5 * jnp.concatenate(pairs, axis=0))
    whole_sum = lines[0] + lines[1]
    upper, lower = high_low(whole_sum)
    extra = jnp.concatenate([upper[:, :DH], lower[:, DH:]], axis=1).astype(BF)
    query_part, proj_part = early[:DH], early[DH:]
    joined = jnp.concatenate([query_part, both_part.astype(BF), proj_part], axis=0)
    for g in range(16):
        for c in range(4):
            parts_out[g, c * 16 : (c + 1) * 16] = joined[
                g * 16 : (g + 1) * 16, c * 128 : (c + 1) * 128
            ]
        parts_out[g, 64:] = extra


def sum_kernel(arrived, share_out, temper_out):
    total = jnp.zeros((72, 128), F32)
    for g in range(16):
        total = total + arrived[g].astype(F32)
    temper_out[...] = jnp.broadcast_to(total[64:, :1] + total[64:, DH : DH + 1], (H, 128))
    share = jnp.concatenate([total[c * 16 : (c + 1) * 16] for c in range(4)], axis=1).astype(BF)
    for k in range(64):
        share_out[k] = share


def output_kernel(core, near, far, gain, wq, wk, wv, gq, gk, gv, gp, gg, turned):
    for which, source in ((core[0], near), (1 - core[0], far)):
        for chip in range(64):
            gx, zl, tx, zh = chip // 16, chip // 8 % 2, chip // 2 % 4, chip % 2
            quarter = tx % 2 * 2 + zh
            start = pl.multiple_of(gx * 128 + which * 64 + quarter * 16, 16)
            turned[zl * 2 + tx // 2, pl.ds(start, 16), :] = source[chip]
    gp[...] = turned[3].astype(F32)
    total = jnp.zeros((D, 1), F32)
    for m, (out, weight) in enumerate(((gq, wq), (gk, wk), (gv, wv))):
        value = turned[m].T.astype(F32)
        out[...] = value
        total = total + jnp.sum(value * weight[...].astype(F32), axis=1, keepdims=True)
    line = jnp.broadcast_to(total, (D, 128)).T
    gg[...] = line[:1] / gain[...]


def finish_kernel(
    site, tok, gain, mq, kv0, kv1, kv2, kv3, wq, wk, wv, wp, layer_out, grad_tok, kv,
):
    for step_y, piece in enumerate((kv0, kv1, kv2, kv3)):
        for step_x in range(4):
            source_x = jnp.bitwise_xor(site[1], step_x)
            source_y = jnp.bitwise_xor(site[2], step_y)
            kv[source_x * 4 + source_y] = piece[step_x]

    def gathered(ref, lanes):
        halves = [
            jnp.concatenate([ref[seat(h, slot), :BLK, lanes] for h in range(H)], axis=1)
            for slot in range(2)
        ]
        return jnp.concatenate(halves, axis=0)

    left, right = slice(0, DH), slice(DH, 2 * DH)
    unit, factor_in, _ = normed_hidden(tok[...], gain[...])
    layer_out[...] = dot_nn(gathered(mq, left), wp[...]).astype(BF)
    query_d, key_d, value_d = gathered(mq, right), gathered(kv, left), gathered(kv, right)
    back_hidden = dot_nt(query_d, wq[...]) + dot_nt(key_d, wk[...]) + dot_nt(value_d, wv[...])
    slope_in = back_hidden * gain[...]
    grad_tok[...] = factor_in * (
        slope_in - unit * jnp.mean(slope_in * unit, axis=-1, keepdims=True)
    )


def whole(shape, dtype):
    return jax.ShapeDtypeStruct(shape, dtype)


def shift(block, step):
    spots = [(t % 2) * 8 + t // 2 for t in range(16)]
    return lax.ppermute(block, RING, [(spots[t], spots[(t + step) % 16]) for t in range(16)])


def swap_cores(block):
    return lax.ppermute(block, "cr", [(0, 1), (1, 0)])


def swap_near(block, axes, step):
    return lax.ppermute(block, axes, [(i, i ^ step) for i in range(4)])


def local(
    tokens, norm_gain, w_query, w_key, w_value, w_proj, temper, neighbours, valid_mask, cotangent
):
    tok = tokens.reshape(ROWS, D)
    cot = cotangent.reshape(ROWS, D)
    gain = norm_gain.reshape(1, D)
    core = lax.axis_index("cr")
    any_spec = pl.BlockSpec(memory_space=pl.ANY)
    smem = pl.BlockSpec(memory_space=pltpu.SMEM)
    hbm = pl.BlockSpec(memory_space=pltpu.HBM)
    vmem = pl.BlockSpec(memory_space=pltpu.VMEM)

    pair = (16, BLK, 2 * DH)
    wide = (16, BLK + EXTRA, 2 * DH)
    kv_send, factors = pl.pallas_call(
        key_kernel,
        cost_estimate=cost(3),
        out_shape=(whole(pair, BF), whole((ROWS, 128), F32)),
        compiler_params=params(56),
    )(tok, gain, w_key, w_value)
    qb_send, rows_send = pl.pallas_call(
        query_kernel,
        cost_estimate=cost(4),
        out_shape=(whole(wide, BF), whole((8, BLK, 2 * D), BF)),
        compiler_params=params(56),
    )(
        tok, gain, cot, neighbours.reshape(2, NB), valid_mask.reshape(2, NB), factors,
        w_query, w_proj,
    )

    own = lax.all_to_all(kv_send, GROUP, 0, 0, tiled=True)
    qb_send, own = lax.optimization_barrier((qb_send, own))
    before = shift(own, 1)
    after = shift(own, -1)
    qb = lax.all_to_all(qb_send, GROUP, 0, 0, tiled=True)
    rows_send, qb, before, after = lax.optimization_barrier((rows_send, qb, before, after))
    rows_near = lax.all_to_all(rows_send, ("gx", "zl"), 0, 0, tiled=True)
    head_id = lax.axis_index("gx") * 2 + core
    temp = temper[head_id] * SCALE
    coef = jnp.stack([temp * math.log2(math.e), temp])

    mq_send, mqt, own_grad, before_grad, after_grad = pl.pallas_call(
        attend_kernel,
        cost_estimate=cost(36),
        out_shape=(
            whole(wide, BF), whole((16, 2 * DH, BLK), BF), whole(pair, F32),
            whole(pair, BF), whole(pair, BF),
        ),
        in_specs=[smem] + [any_spec] * 3 + [vmem],
        out_specs=tuple([hbm] * 5),
        scratch_shapes=[
            pltpu.VMEM(wide, BF),
            pltpu.VMEM((16, 2 * DH, BLK), BF),
            pltpu.VMEM(pair, BF),
            pltpu.VMEM(pair, BF),
            pltpu.VMEM((16, 3, BLK, 2 * DH), BF),
            pltpu.VMEM((16, 2 * DH, 3 * BLK), BF),
            pltpu.VMEM((16, 3, BLK, 2 * DH), F32),
            pltpu.VMEM((NB * BLK, 2 * BLK), F32),
            pltpu.VMEM((NB * BLK, 2 * BLK), F32),
            pltpu.VMEM((16, 128), F32),
            pltpu.SMEM((16, 128), F32),
            pltpu.SemaphoreType.DMA((9,)),
        ],
        compiler_params=params(60),
    )(coef, own, before, after, qb)
    from_after = shift(before_grad, -1)
    from_before = shift(after_grad, 1)
    rows_near, mq_send = lax.optimization_barrier((rows_near, mq_send))
    rows_far = swap_cores(rows_near)
    mq = lax.all_to_all(mq_send, GROUP, 0, 0, tiled=True)
    site = jnp.stack([core, lax.axis_index("gx"), lax.axis_index("zl") * 2 + core])
    early = pl.pallas_call(
        early_kernel,
        cost_estimate=cost(3),
        out_shape=whole((2 * DH, D), BF),
        in_specs=[smem] + [vmem] * 3,
        compiler_params=params(10),
    )(site, mqt, rows_near, rows_far)
    hidden_spec = pl.BlockSpec((8, BLK, D), lambda i: (0, 0, 0))

    def one_spec(array):
        return pl.BlockSpec(array.shape, lambda i: (0,) * array.ndim)

    kv_back, parts = pl.pallas_call(
        head_kernel,
        cost_estimate=cost(7),
        out_shape=(whole((4, 4, BLK, 2 * DH), BF), whole((16, 72, 128), BF)),
        grid=(1,),
        in_specs=[smem]
        + [one_spec(a) for a in (own_grad, from_after, from_before, own, qb, early, mq)]
        + [hidden_spec, hidden_spec],
        scratch_shapes=[pltpu.VMEM((16, 2 * DH, BLK), BF)],
        compiler_params=params(56),
    )(site, own_grad, from_after, from_before, own, qb, early, mq, rows_near, rows_far)
    arrived = lax.all_to_all(parts, RING, 0, 0, tiled=True)
    turn = [kv_back[0]] + [swap_near(kv_back[step], "gx", step) for step in range(1, 4)]
    share, temper_sum = pl.pallas_call(
        sum_kernel,
        cost_estimate=cost(2),
        out_shape=(whole((64, 16, D), BF), whole((H, 128), F32)),
        compiler_params=params(6),
    )(arrived)
    near = lax.all_to_all(share, CHIPS, 0, 0, tiled=True)
    kv = [jnp.stack([piece[step] for piece in turn]) for step in range(4)]
    grad_temper = temper_sum[:, 0] / (temper * math.log2(math.e))
    kv[1], grad_temper = lax.optimization_barrier((kv[1], grad_temper))
    kv = [kv[0]] + [swap_near(kv[step], ("zl", "cr"), step) for step in range(1, 4)]
    near, *kv = lax.optimization_barrier((near, *kv))
    layer_out, grad_tokens = pl.pallas_call(
        finish_kernel,
        cost_estimate=cost(4),
        out_shape=(whole((ROWS, D), BF), whole((ROWS, D), F32)),
        in_specs=[smem] + [vmem] * 11,
        scratch_shapes=[pltpu.VMEM(pair, BF)],
        compiler_params=params(56),
    )(site, tok, gain, mq, *kv, w_query, w_key, w_value, w_proj)
    far = swap_cores(near)
    square = whole((D, D), F32)
    gq, gk, gv, gp, grad_gain = pl.pallas_call(
        output_kernel,
        cost_estimate=cost(5),
        out_shape=(square, square, square, square, whole((1, D), F32)),
        in_specs=[smem] + [vmem] * 6,
        scratch_shapes=[pltpu.VMEM((4, D, D), BF)],
        compiler_params=params(16),
    )(core.reshape(1), near, far, gain, w_query, w_key, w_value)
    return (
        layer_out.reshape(tokens.shape),
        grad_tokens.reshape(tokens.shape),
        grad_gain.reshape(D),
        gq,
        gk,
        gv,
        gp,
        grad_temper,
    )


def solution(mesh):
    fine = Mesh(mesh.devices.reshape(4, 2, 2, 4, 2), ALL)
    lattice = ("gx", ("zl", "cr"), ("tx", "zh"))
    blocks = P(*lattice, None, None)
    lists = P(*lattice, None)
    return jax.shard_map(
        local,
        mesh=fine,
        in_specs=(blocks, P(), P(), P(), P(), P(), P(), lists, lists, blocks),
        out_specs=(blocks, blocks, P(), P(), P(), P(), P(), P()),
        check_vma=False,
    )
```
